256 devices in a mesh: lat: 64 (over z_lo, y, x), depth: 4 (over z_hi, core).
Axes of the slice: x: 4, y: 4, z: 8 (z_hi: 2, z_lo: 4; z = z_hi * 4 + z_lo), core: 2. Of those that a mesh axis runs over, the one named last changes fastest.
Arguments:
- velocity_fine: float32 [3, 768, 64, 384], P(None, 'lat', 'depth'), may hold values from -6 to 6
- stress_fine: float32 [6, 768, 64, 384], P(None, 'lat', 'depth'), may hold values from -6 to 6
- memory_fine: float32 [6, 768, 64, 384], P(None, 'lat', 'depth'), may hold values from -1.8 to 1.8
- peak_fine: float32 [768, 64, 384], P('lat', 'depth'), may hold values from 0 to 12
- zone_fine: int32 [768, 64, 384], P('lat', 'depth'), may hold values from 0 to 7
- velocity_coarse: float32 [3, 256, 128, 128], P(None, 'lat', 'depth'), may hold values from -6 to 6
- stress_coarse: float32 [6, 256, 128, 128], P(None, 'lat', 'depth'), may hold values from -6 to 6
- memory_coarse: float32 [6, 256, 128, 128], P(None, 'lat', 'depth'), may hold values from -1.8 to 1.8
- peak_coarse: float32 [256, 128, 128], P('lat', 'depth'), may hold values from 0 to 12
- zone_coarse: int32 [256, 128, 128], P('lat', 'depth'), may hold values from 0 to 7
- zone_table: float32 [8, 5], replicated, may hold values from 0.05 to 1, as said below
- interp_weight: int32 [2, 3], replicated, may hold values from 0 to 8
- restrict_weight: int32 [2, 3], replicated, may hold values from 1 to 8
Outputs:
- fine_velocity: float32 [3, 768, 64, 384], P(None, 'lat', 'depth')
- fine_stress: float32 [6, 768, 64, 384], P(None, 'lat', 'depth')
- fine_memory: float32 [6, 768, 64, 384], P(None, 'lat', 'depth')
- fine_peak: float32 [768, 64, 384], P('lat', 'depth')
- coarse_velocity: float32 [3, 256, 128, 128], P(None, 'lat', 'depth')
- coarse_stress: float32 [6, 256, 128, 128], P(None, 'lat', 'depth')
- coarse_memory: float32 [6, 256, 128, 128], P(None, 'lat', 'depth')
- coarse_peak: float32 [256, 128, 128], P('lat', 'depth')
The draws below stay inside these ranges and needn't reach their ends.
Inputs may be any that keep to these rules, and one draw needn't show every extreme that they name: `zone_table`: column 0 lies in 0.5 to 1, columns 1 and 2 in 0.1 to 0.3, column 3 in 0.5 to 0.95, column 4 in 0.05 to 0.3.
All inputs are finite; a program needn't handle non-finite values.
Results may differ from the reference program's by a relative error of at most 0.0003.
Values sent between devices are 32-bit elements; how exact they have to be, the bound alone decides.
No kernel may reach another device: no remote copies, remote signals or barrier semaphores. Data moves between devices by JAX's collectives and lax.ppermute only.
A program may use at most 128 MiB of HBM per device.

```python
import jax
import jax.numpy as jnp
from jax import lax

NYC = 128
ZONES = 8
STEPS = 2
NYF = 384
NXC = 256
NXF = 768
NZF = 64
NZC = 128


def draw_zone_table(key, part):
    lower_edge = jnp.array([0.5, 0.1, 0.1, 0.5, 0.05], jnp.float32)
    upper_edge = jnp.array([1.0, 0.3, 0.3, 0.95, 0.3], jnp.float32)
    unit = jax.random.uniform(jax.random.fold_in(key, 17), (ZONES, 5), jnp.float32)
    return lower_edge + (upper_edge - lower_edge) * unit


def with_ends(values, rng, least, largest):
    extent = values.shape
    spot = [jax.random.randint(jax.random.fold_in(rng, axis), (), 0, extent[axis]) for axis in range(len(extent))]
    values = values.at[tuple(spot)].set(least)
    longest = extent.index(max(extent))
    spot[longest] = (spot[longest] + 1) % extent[longest]
    return values.at[tuple(spot)].set(largest)


def levels(stream_key, shape, pieces, low, high):
    factor_of, own = 1.0, jax.random.fold_in(stream_key, 6)
    for dim, blocks in pieces:
        draws = jnp.exp(jax.random.uniform(jax.random.fold_in(own, dim), (blocks,), jnp.float32, low / len(pieces), high / len(pieces)))
        factor_of = factor_of * jnp.repeat(draws, shape[dim] // blocks).reshape([-1 if axis == dim else 1 for axis in range(len(shape))])
    return factor_of


def noise(key, dims, scale, limit, cuts=(), kind=jnp.bfloat16):
    drawn = jax.random.normal(key, dims, jnp.float32) * scale
    if len(cuts) > 0:
        drawn = levels(key, dims, cuts, -0.22, 0.18) * drawn
    return jnp.clip(drawn, min=-limit, max=limit).astype(kind)


def setup_inputs(seed: int = 0) -> dict:
    seeds = jax.random.split(jax.random.key(seed), 14)
    return {
        "velocity_fine": noise(seeds[0], (3, NXF, NZF, NYF), 1.0, 6.0, ((1, 64), (2, 4)), jnp.float32),
        "stress_fine": noise(seeds[1], (6, NXF, NZF, NYF), 1.0, 6.0, ((1, 64), (2, 4)), jnp.float32),
        "memory_fine": noise(seeds[2], (6, NXF, NZF, NYF), 0.3, 1.8, ((1, 64), (2, 4)), jnp.float32),
        "peak_fine": jnp.clip(12.0 * jax.random.uniform(seeds[3], (NXF, NZF, NYF), jnp.float32) ** levels(seeds[3], (NXF, NZF, NYF), ((0, 64), (1, 4)), -0.2, 0.2), 0.0, 12.0),
        "zone_fine": with_ends(jax.random.randint(seeds[4], (NXF, NZF, NYF), 0, ZONES), jax.random.fold_in(seeds[4], 1), 0, ZONES - 1).astype(jnp.int32),
        "velocity_coarse": noise(seeds[5], (3, NXC, NZC, NYC), 1.0, 6.0, ((1, 64), (2, 4)), jnp.float32),
        "stress_coarse": noise(seeds[6], (6, NXC, NZC, NYC), 1.0, 6.0, ((1, 64), (2, 4)), jnp.float32),
        "memory_coarse": noise(seeds[7], (6, NXC, NZC, NYC), 0.3, 1.8, ((1, 64), (2, 4)), jnp.float32),
        "peak_coarse": jnp.clip(12.0 * jax.random.uniform(seeds[8], (NXC, NZC, NYC), jnp.float32) ** levels(seeds[8], (NXC, NZC, NYC), ((0, 64), (1, 4)), -0.2, 0.2), 0.0, 12.0),
        "zone_coarse": with_ends(jax.random.randint(seeds[9], (NXC, NZC, NYC), 0, ZONES), jax.random.fold_in(seeds[9], 1), 0, ZONES - 1).astype(jnp.int32),
        "zone_table": draw_zone_table(jax.random.fold_in(seeds[13], 71), 0),
        "interp_weight": with_ends(jax.random.randint(seeds[11], (2, 3), 0, 9), jax.random.fold_in(seeds[11], 1), 0, 8).astype(jnp.int32),
        "restrict_weight": with_ends(jax.random.randint(seeds[12], (2, 3), 1, 9), jax.random.fold_in(seeds[12], 1), 1, 8).astype(jnp.int32),
    }


time_step = 0.4
near_coef = 9.0 / 8.0
far_coef = 1.0 / 24.0

def shifted(field, axis, offset):
    index = [slice(None), slice(2, -2), slice(2, -2), slice(2, -2)]
    index[axis] = slice(2 + offset, field.shape[axis] - 2 + offset)
    return field[tuple(index)]

def forward(field, axis):
    return near_coef * (shifted(field, axis, 1) - shifted(field, axis, 0)) - far_coef * (shifted(field, axis, 2) - shifted(field, axis, -1))

def backward(field, axis):
    return near_coef * (shifted(field, axis, 0) - shifted(field, axis, -1)) - far_coef * (shifted(field, axis, 1) - shifted(field, axis, -2))

def materials(zone, zone_table):
    columns = []
    for column in range(5):
        value = jnp.zeros(zone.shape, jnp.float32)
        for level in range(zone_table.shape[0]):
            value = jnp.where(zone == level, zone_table[level, column], value)
        columns.append(value)
    return columns

def velocity_update(padded, velocity, buoyancy, spacing):

    def part(index):
        return padded[index:index + 1]
    accel_x = forward(part(0), 1) + backward(part(3), 3) + backward(part(4), 2)
    accel_y = backward(part(3), 1) + forward(part(1), 3) + backward(part(5), 2)
    accel_z = backward(part(4), 1) + backward(part(5), 3) + forward(part(2), 2)
    accel = jnp.concatenate([accel_x, accel_y, accel_z], axis=0)
    return velocity + time_step / spacing * buoyancy[None] * accel

def stress_update(padded, stress, memory, props, spacing):
    lame, shear, decay, damping = (props[1][None], props[2][None], props[3][None], props[4][None])

    def part(index):
        return padded[index:index + 1]
    normal_x = backward(part(0), 1)
    normal_y = backward(part(1), 3)
    normal_z = backward(part(2), 2)
    shear_xy = 0.5 * (forward(part(0), 3) + forward(part(1), 1))
    shear_xz = 0.5 * (forward(part(0), 2) + forward(part(2), 1))
    shear_yz = 0.5 * (forward(part(1), 2) + forward(part(2), 3))
    volume = normal_x + normal_y + normal_z
    rate = jnp.concatenate([lame * volume + 2.0 * shear * normal_x, lame * volume + 2.0 * shear * normal_y, lame * volume + 2.0 * shear * normal_z, 2.0 * shear * shear_xy, 2.0 * shear * shear_xz, 2.0 * shear * shear_yz], axis=0) / spacing
    memory_next = decay * memory - damping * (1.0 - decay) * rate
    stress_next = stress + time_step * (rate + 0.5 * (memory + memory_next))
    return (stress_next, memory_next)

def entry_key(first, second):
    return (min(first, second), max(first, second))

def rotate(entries, first, second):
    other = 3 - first - second
    pivot = entries[first, second]
    gap = entries[second, second] - entries[first, first]
    denominator = jnp.abs(gap) + jnp.sqrt(gap * gap + 4.0 * pivot * pivot)
    direction = jnp.where(gap >= 0, 1.0, -1.0)
    usable = denominator > 0
    tangent = jnp.where(usable, 2.0 * pivot * direction / jnp.where(usable, denominator, 1.0), 0.0)
    cosine = 1.0 / jnp.sqrt(1.0 + tangent * tangent)
    sine = tangent * cosine
    low_entry = entries[entry_key(other, first)]
    high_entry = entries[entry_key(other, second)]
    result = dict(entries)
    result[first, first] = entries[first, first] - tangent * pivot
    result[second, second] = entries[second, second] + tangent * pivot
    result[first, second] = jnp.zeros_like(pivot)
    result[entry_key(other, first)] = cosine * low_entry - sine * high_entry
    result[entry_key(other, second)] = sine * low_entry + cosine * high_entry
    return result

def strain_peak(stress, props, peak):
    lame, shear = (props[1], props[2])
    trace = stress[0] + stress[1] + stress[2]
    isotropic = lame * trace / (3.0 * lame + 2.0 * shear)
    scale = 0.5 / shear
    entries = {(0, 0): (stress[0] - isotropic) * scale, (1, 1): (stress[1] - isotropic) * scale, (2, 2): (stress[2] - isotropic) * scale, (0, 1): stress[3] * scale, (0, 2): stress[4] * scale, (1, 2): stress[5] * scale}
    for sweep in range(3):
        entries = rotate(entries, 0, 1)
        entries = rotate(entries, 0, 2)
        entries = rotate(entries, 1, 2)
    principal = jnp.maximum(jnp.maximum(entries[0, 0], entries[1, 1]), entries[2, 2])
    return jnp.maximum(peak, principal)

def make_tables(interp_weight, restrict_weight, coarse_cells):
    x_share = interp_weight[0].astype(jnp.float32) / 8.0
    y_share = interp_weight[1].astype(jnp.float32) / 8.0
    x_weight = restrict_weight[0].astype(jnp.float32)
    y_weight = restrict_weight[1].astype(jnp.float32)
    coarse_index = lax.broadcasted_iota(jnp.int32, (coarse_cells, 3 * coarse_cells), 0)
    fine_index = lax.broadcasted_iota(jnp.int32, (coarse_cells, 3 * coarse_cells), 1)
    phase = fine_index % 3
    block = fine_index // 3
    y_interp = jnp.where(phase == 0, y_share[0], jnp.where(phase == 1, y_share[1], y_share[2]))
    y_restrict = jnp.where(phase == 0, y_weight[0], jnp.where(phase == 1, y_weight[1], y_weight[2]))
    y_spread = jnp.where(coarse_index == block, y_interp, 0.0) + jnp.where(coarse_index == block + 1, 1.0 - y_interp, 0.0)
    y_gather = jnp.where(coarse_index == block, y_restrict, 0.0).T
    normaliser = 3.0 * jnp.sum(x_weight) * jnp.sum(y_weight)
    return (x_share, y_spread, x_weight, y_gather, normaliser)

def interpolate(planes, tables):
    x_share, y_spread = (tables[0], tables[1])
    upper = planes[:, :, 0:1]
    lower = planes[:, :, 1:2]
    layered = jnp.concatenate([(2.0 * upper + lower) / 3.0, (upper + 2.0 * lower) / 3.0], axis=2)
    share = x_share[None, None, :, None, None]
    across = share * layered[:, :-1, None] + (1.0 - share) * layered[:, 1:, None]
    count, rows = (across.shape[0], across.shape[1])
    flat = across.reshape(count * rows * 6, -1)
    spread = jnp.dot(flat, y_spread, precision=lax.Precision.HIGHEST)
    return spread.reshape(count, rows * 3, 2, -1)

def restrict(block, tables):
    x_weight, y_gather, normaliser = (tables[2], tables[3], tables[4])
    count, rows = (block.shape[0], block.shape[1])
    layers = lax.optimization_barrier(jnp.sum(block.reshape(count, rows, 2, 3, -1), axis=3))
    grouped = layers.reshape(count, rows // 3, 3, 2, -1)
    across = lax.optimization_barrier(jnp.sum(x_weight[None, None, :, None, None] * grouped, axis=2))
    flat = across.reshape(count * (rows // 3) * 2, -1)
    gathered = jnp.dot(flat, y_gather, precision=lax.Precision.HIGHEST)
    return gathered.reshape(count, rows // 3, 2, -1) / normaliser

def pad_fine(fine, coarse, tables):
    planes = jnp.pad(coarse[:, :, 0:2], ((0, 0), (0, 1), (0, 0), (0, 0)))
    ghost = interpolate(planes, tables)
    column = jnp.concatenate([jnp.zeros_like(fine[:, :, 0:2]), fine, ghost], axis=2)
    return jnp.pad(column, ((0, 0), (2, 2), (0, 0), (2, 2)))

def pad_coarse(coarse, fine, tables):
    ghost = restrict(fine[:, :, -6:], tables)
    column = jnp.concatenate([ghost, coarse, jnp.zeros_like(coarse[:, :, 0:2])], axis=2)
    return jnp.pad(column, ((0, 0), (2, 2), (0, 0), (2, 2)))

def reference(velocity_fine, stress_fine, memory_fine, peak_fine, zone_fine, velocity_coarse, stress_coarse, memory_coarse, peak_coarse, zone_coarse, zone_table, interp_weight, restrict_weight):
    tables = make_tables(interp_weight, restrict_weight, stress_coarse.shape[3])
    props_fine = materials(zone_fine, zone_table)
    props_coarse = materials(zone_coarse, zone_table)
    for step in range(STEPS):
        padded_fine = pad_fine(stress_fine, stress_coarse, tables)
        padded_coarse = pad_coarse(stress_coarse, stress_fine, tables)
        velocity_fine = velocity_update(padded_fine, velocity_fine, props_fine[0], 1.0)
        velocity_coarse = velocity_update(padded_coarse, velocity_coarse, props_coarse[0], 3.0)
        padded_fine = pad_fine(velocity_fine, velocity_coarse, tables)
        padded_coarse = pad_coarse(velocity_coarse, velocity_fine, tables)
        stress_fine, memory_fine = stress_update(padded_fine, stress_fine, memory_fine, props_fine, 1.0)
        stress_coarse, memory_coarse = stress_update(padded_coarse, stress_coarse, memory_coarse, props_coarse, 3.0)
        peak_fine = strain_peak(stress_fine, props_fine, peak_fine)
        peak_coarse = strain_peak(stress_coarse, props_coarse, peak_coarse)
    return (velocity_fine, stress_fine, memory_fine, peak_fine, velocity_coarse, stress_coarse, memory_coarse, peak_coarse)
```

```python
import functools

import jax
import jax.numpy as jnp
from jax import lax
from jax.experimental import pallas as pl
from jax.experimental.pallas import tpu as pltpu
from jax.sharding import PartitionSpec as P

STEPS = 2
DT = 0.4
NEAR = 9.0 / 8.0
FAR = 1.0 / 24.0
TINY = 1e-36

STRESS_X = ([(0, 1), (3, 2), (3, 1), (4, 2), (4, 1)], [(0, 0), (0, 1), (3, 0), (4, 0)])
STRESS_Z = ([(4, 2), (4, 1), (5, 2), (5, 1), (2, 1)], [(4, 0), (5, 0), (2, 0), (2, 1)])
VELOCITY_X = ([(0, 2), (0, 1), (1, 1), (2, 1)], [(0, 0), (1, 0), (1, 1), (2, 0), (2, 1)])
VELOCITY_Z = ([(2, 2), (2, 1), (0, 1), (1, 1)], [(2, 0), (0, 0), (0, 1), (1, 0), (1, 1)])

CB, LAME, MU2, DECAY, DAMP, ISO, SCALE = range(7)


class Sizes:
    def __init__(self, fine, coarse):
        self.fx, self.fz, self.fy = fine
        self.cx, self.cz, self.cy = coarse
        self.lanes = self.fy // self.cy
        self.lat_fine = 5 * self.fz
        self.lat_rows = self.lat_fine + -(-5 // self.lanes) * self.cz
        self.dep_fine = 5 * self.fx
        used = self.dep_fine + 5 * -(-self.cx // self.lanes)
        self.dep_rows = -(-used // 8) * 8

    def lat_slot(self, k):
        row = self.lat_fine + (k // self.lanes) * self.cz
        lane = (k % self.lanes) * self.cy
        return (slice(row, row + self.cz), slice(lane, lane + self.cy))

    def dep_slot(self, k, x):
        row = self.dep_fine + (x // self.lanes) * 5 + k
        lane = (x % self.lanes) * self.cy
        return (slice(row, row + 1), slice(lane, lane + self.cy))


def y_shift(f, offset, lane):
    width = f.shape[1]
    moved = pltpu.roll(f, (-offset) % width, 1)
    inside = lane < width - offset if offset > 0 else lane >= -offset
    return jnp.where(inside, moved, 0.0)


def z_shift(f, offset, row, low, high):
    depth = f.shape[0]
    moved = pltpu.roll(f, (-offset) % depth, 0)
    if offset < 0:
        for j in range(-offset):
            moved = jnp.where(row == j, low[offset + j], moved)
    else:
        for j in range(offset):
            moved = jnp.where(row == depth - offset + j, high[j], moved)
    return moved


def y_parts(f, up, lane):
    if up:
        return y_shift(f, 1, lane) - f, y_shift(f, 2, lane) - y_shift(f, -1, lane)
    return f - y_shift(f, -1, lane), y_shift(f, 1, lane) - y_shift(f, -2, lane)


def z_parts(f, up, row, low, high):
    def at(offset):
        return z_shift(f, offset, row, low, high)

    if up:
        return at(1) - f, at(2) - at(-1)
    return f - at(-1), at(1) - at(-2)


def x_parts(get, x, up):
    if up:
        return get(x + 1) - get(x), get(x + 2) - get(x - 1)
    return get(x) - get(x - 1), get(x + 1) - get(x - 2)


class Grid:
    def __init__(self, sizes, fine, field, x_lists, z_lists, xlo, xhi, zlo, zhi):
        self.sizes, self.fine, self.field = sizes, fine, field
        self.x_lists, self.z_lists = x_lists, z_lists
        self.xlo, self.xhi, self.zlo, self.zhi = xlo, xhi, zlo, zhi
        self.nx = sizes.fx if fine else sizes.cx
        self.nz = sizes.fz if fine else sizes.cz
        self.ny = sizes.fy if fine else sizes.cy
        self.row = lax.broadcasted_iota(jnp.int32, (self.nz, self.ny), 0)
        self.lane = lax.broadcasted_iota(jnp.int32, (self.nz, self.ny), 1)

    def x_layer(self, ref, k):
        if self.fine:
            return ref[k * self.nz : (k + 1) * self.nz, :]
        return ref[self.sizes.lat_slot(k)]

    def x_get(self, comp):
        def get(x):
            if isinstance(x, int) and x < 0:
                return self.x_layer(self.xlo, self.x_lists[0].index((comp, -x)))
            if isinstance(x, int) and x >= self.nx:
                return self.x_layer(self.xhi, self.x_lists[1].index((comp, x - self.nx)))
            return self.field[comp, x]

        return get

    def z_row(self, ref, k, x):
        if not self.fine:
            return ref[self.sizes.dep_slot(k, x)]
        if isinstance(x, int):
            return ref[k * self.nx + x : k * self.nx + x + 1, :]
        return ref[pl.ds(k * self.nx + x, 1), :]

    def z_halo(self, comp, x):
        low = {-r: self.z_row(self.zlo, k, x) for k, (c, r) in enumerate(self.z_lists[0]) if c == comp}
        high = {r: self.z_row(self.zhi, k, x) for k, (c, r) in enumerate(self.z_lists[1]) if c == comp}
        return low, high

    def dx(self, comp, x, up):
        return x_parts(self.x_get(comp), x, up)

    def dy(self, comp, x, up):
        return y_parts(self.field[comp, x], up, self.lane)

    def dz(self, comp, x, up):
        low, high = self.z_halo(comp, x)
        return z_parts(self.field[comp, x], up, self.row, low, high)

    def rows(self, body):
        if self.nx > 8:

            def step(x, carry):
                body(x)
                return carry

            for x in (0, 1):
                body(x)
            lax.fori_loop(2, self.nx - 2, step, 0)
            for x in (self.nx - 2, self.nx - 1):
                body(x)
        else:
            for x in range(self.nx):
                body(x)


def combine(*parts):
    near = functools.reduce(lambda a, b: a + b, [p[0] for p in parts])
    far = functools.reduce(lambda a, b: a + b, [p[1] for p in parts])
    return NEAR * near - FAR * far


def velocity_rows(grid, velocity, out, props):
    scale = DT if grid.fine else DT / 3.0

    def body(x):
        speed = scale * props[CB, x]
        ax = combine(grid.dx(0, x, True), grid.dy(3, x, False), grid.dz(4, x, False))
        out[0, x] = velocity[0, x] + speed * ax
        ay = combine(grid.dx(3, x, False), grid.dy(1, x, True), grid.dz(5, x, False))
        out[1, x] = velocity[1, x] + speed * ay
        az = combine(grid.dx(4, x, False), grid.dy(5, x, False), grid.dz(2, x, True))
        out[2, x] = velocity[2, x] + speed * az

    grid.rows(body)


def stress_rows(grid, stress, memory, stress_out, memory_out, props):
    inverse = 1.0 if grid.fine else 1.0 / 3.0

    def body(x):
        lame, twice = props[LAME, x], props[MU2, x]
        decay, damp = props[DECAY, x], props[DAMP, x]
        if inverse != 1.0:
            lame, twice = lame * inverse, twice * inverse
        half = 0.5 * twice

        def finish(comp, rate):
            old = memory[comp, x]
            new = decay * old - damp * rate
            memory_out[comp, x] = new
            stress_out[comp, x] = stress[comp, x] + DT * (rate + 0.5 * (old + new))

        xx = combine(grid.dx(0, x, False))
        yy = combine(grid.dy(1, x, False))
        zz = combine(grid.dz(2, x, False))
        volume = lame * (xx + yy + zz)
        finish(0, volume + twice * xx)
        finish(1, volume + twice * yy)
        finish(2, volume + twice * zz)
        finish(3, half * combine(grid.dy(0, x, True), grid.dx(1, x, True)))
        finish(4, half * combine(grid.dz(0, x, True), grid.dx(2, x, True)))
        finish(5, half * combine(grid.dz(1, x, True), grid.dy(2, x, True)))

    grid.rows(body)


def receive(sizes, place, latE, latO, depE, depO, diag, z_lists, weights, xlo, xhi, zlo, zhi, lift):
    lat, depth = place[0], place[1]
    lat_even, depth_even = lax.rem(lat, 2) == 0, lax.rem(depth, 2) == 0
    last_lat, last_depth = place[2] - 1, place[3] - 1

    @pl.when(lat_even)
    def _():
        xlo[...] = latO[...]
        xhi[...] = latE[...]

    @pl.when(jnp.logical_not(lat_even))
    def _():
        xlo[...] = latE[...]
        xhi[...] = latO[...]

    @pl.when(lat == 0)
    def _():
        xlo[...] = jnp.zeros_like(xlo)

    @pl.when(lat == last_lat)
    def _():
        xhi[...] = jnp.zeros_like(xhi)

    @pl.when(depth_even)
    def _():
        zlo[...] = depO[...]
        zhi[...] = depE[...]

    @pl.when(jnp.logical_not(depth_even))
    def _():
        zlo[...] = depE[...]
        zhi[...] = depO[...]

    @pl.when(depth == 0)
    def _():
        zlo[0 : sizes.dep_fine, :] = jnp.zeros((sizes.dep_fine, sizes.fy), jnp.float32)

    @pl.when(depth == last_depth)
    def _():
        interp = weights
        count = len(z_lists[1])
        lift[...] = jnp.zeros_like(lift)
        beyond = jnp.where(lat == last_lat, 0.0, 1.0)
        for k in range(count):
            planes = [depO[sizes.dep_slot(k, a)] for a in range(sizes.cx)]
            planes.append(diag[k : k + 1, :] * beyond)
            for a in range(sizes.cx):
                for p in range(3):
                    share = interp[0, p].astype(jnp.float32) * 0.125
                    x = k * sizes.fx + 3 * a + p
                    lift[x : x + 1, :] = share * planes[a] + (1.0 - share) * planes[a + 1]
        c = lax.broadcasted_iota(jnp.int32, (sizes.cy, sizes.fy), 0)
        f = lax.broadcasted_iota(jnp.int32, (sizes.cy, sizes.fy), 1)
        gap = f - 3 * c
        spread = jnp.zeros((sizes.cy, sizes.fy), jnp.float32)
        for p in range(3):
            share = interp[1, p].astype(jnp.float32) * 0.125
            spread = jnp.where(gap == p, share, spread)
            spread = jnp.where(gap == p - 3, 1.0 - share, spread)
        ghost = jnp.dot(
            lift[...], spread, precision=lax.Precision.HIGHEST, preferred_element_type=jnp.float32
        )
        zhi[...] = jnp.zeros_like(zhi)
        zhi[0 : sizes.dep_fine, :] = ghost[0 : sizes.dep_fine, :]


def send(sizes, place, fine, coarse, x_lists, z_lists, weights, latE, latO, depE, depO, diag, gather):
    lat, depth = place[0], place[1]
    lat_even, depth_even = lax.rem(lat, 2) == 0, lax.rem(depth, 2) == 0
    last_depth = place[3] - 1

    def pack_x(up, down):
        for ref, entries, high in ((up, x_lists[0], True), (down, x_lists[1], False)):
            for k, (comp, r) in enumerate(entries):
                ref[k * sizes.fz : (k + 1) * sizes.fz, :] = fine[comp, sizes.fx - r if high else r]
                ref[sizes.lat_slot(k)] = coarse[comp, sizes.cx - r if high else r]

    def pack_z(up, down):
        for ref, entries, high in ((up, z_lists[0], True), (down, z_lists[1], False)):
            for k, (comp, r) in enumerate(entries):
                z = sizes.fz - r if high else r
                for x in range(sizes.fx):
                    ref[k * sizes.fx + x : k * sizes.fx + x + 1, :] = fine[comp, x, z : z + 1, :]
                z = sizes.cz - r if high else r
                for x in range(sizes.cx):
                    ref[sizes.dep_slot(k, x)] = coarse[comp, x, z : z + 1, :]

    @pl.when(lat_even)
    def _():
        pack_x(latE, latO)

    @pl.when(jnp.logical_not(lat_even))
    def _():
        pack_x(latO, latE)

    @pl.when(depth_even)
    def _():
        pack_z(depE, depO)

    @pl.when(jnp.logical_not(depth_even))
    def _():
        pack_z(depO, depE)

    diag[...] = jnp.zeros_like(diag)

    @pl.when(depth == 0)
    def _():
        for k, (comp, j) in enumerate(z_lists[1]):
            for x in range(sizes.cx):
                plane = ((2.0 - j) * coarse[comp, x, 0:1, :] + (1.0 + j) * coarse[comp, x, 1:2, :]) / 3.0
                depO[sizes.dep_slot(k, x)] = plane
                if x == 0:
                    diag[k : k + 1, :] = plane

    @pl.when(depth == last_depth)
    def _():
        restrict = weights
        wx = [restrict[0, p].astype(jnp.float32) for p in range(3)]
        wy = [restrict[1, p].astype(jnp.float32) for p in range(3)]
        gather[...] = jnp.zeros_like(gather)
        for k, (comp, r) in enumerate(z_lists[0]):
            z = sizes.fz - 3 * r
            for a in range(sizes.cx):
                total = None
                for p in range(3):
                    f = fine[comp, 3 * a + p, z : z + 3, :]
                    layers = wx[p] * (f[0:1] + f[1:2] + f[2:3])
                    total = layers if total is None else total + layers
                row = k * sizes.cx + a
                gather[row : row + 1, :] = total
        f = lax.broadcasted_iota(jnp.int32, (sizes.fy, sizes.cy), 0)
        c = lax.broadcasted_iota(jnp.int32, (sizes.fy, sizes.cy), 1)
        gap = f - 3 * c
        table = jnp.zeros((sizes.fy, sizes.cy), jnp.float32)
        for p in range(3):
            table = jnp.where(gap == p, wy[p], table)
        summed = jnp.dot(
            gather[...], table, precision=lax.Precision.HIGHEST, preferred_element_type=jnp.float32
        )
        norm = jnp.full((1, sizes.cy), 3.0 * (wx[0] + wx[1] + wx[2]) * (wy[0] + wy[1] + wy[2]))
        lifted = summed / norm
        for k in range(len(z_lists[0])):
            for a in range(sizes.cx):
                row = k * sizes.cx + a
                depO[sizes.dep_slot(k, a)] = lifted[row : row + 1, :]


SMEM = pl.BlockSpec(memory_space=pltpu.SMEM)
VMEM = pl.BlockSpec(memory_space=pltpu.VMEM)
LIMIT = 48 * 1024 * 1024


def packs(sizes):
    lat = jax.ShapeDtypeStruct((sizes.lat_rows, sizes.fy), jnp.float32)
    dep = jax.ShapeDtypeStruct((sizes.dep_rows, sizes.fy), jnp.float32)
    return [lat, lat, dep, dep, jax.ShapeDtypeStruct((8, sizes.cy), jnp.float32)]


def halo_scratch(sizes):
    lat = pltpu.VMEM((sizes.lat_rows, sizes.fy), jnp.float32)
    dep = pltpu.VMEM((sizes.dep_rows, sizes.fy), jnp.float32)
    return [lat, lat, dep, dep, pltpu.VMEM((-(-sizes.dep_fine // 8) * 8, sizes.cy), jnp.float32)]


def gather_scratch(sizes):
    return pltpu.VMEM((-(-5 * sizes.cx // 8) * 8, sizes.fy), jnp.float32)


def like(x):
    return jax.ShapeDtypeStruct(x.shape, x.dtype)


def call(kernel, name, smem, vmem, outs, scratch, work):
    moved = sum(x.size * 4 for x in vmem) + sum(4 * o.size for o in outs)
    return pl.pallas_call(
        kernel,
        name=name,
        out_shape=outs,
        in_specs=[SMEM] * len(smem) + [VMEM] * len(vmem),
        out_specs=[VMEM] * len(outs),
        scratch_shapes=scratch,
        compiler_params=pltpu.CompilerParams(vmem_limit_bytes=LIMIT),
        cost_estimate=pl.CostEstimate(flops=work, bytes_accessed=moved, transcendentals=0),
    )(*smem, *vmem)


def pack_stress(sizes, place, restrict, fine, coarse):
    def kernel(place, restrict, fine, coarse, latE, latO, depE, depO, diag, gather):
        send(sizes, place, fine, coarse, STRESS_X, STRESS_Z, restrict, latE, latO, depE, depO, diag, gather)

    return call(
        kernel, "pack_stress", (place, restrict), (fine, coarse), packs(sizes), [gather_scratch(sizes)], 10**6
    )


def materials(table, zone_fine, zone_coarse):
    def kernel(table, zone_fine, zone_coarse, fine, coarse):
        for zone_ref, out in ((zone_fine, fine), (zone_coarse, coarse)):

            def step(x, carry, zone_ref=zone_ref, out=out):
                zone = zone_ref[x]
                for column in range(7):
                    value = jnp.full(zone.shape, table[7, column])
                    for level in range(7):
                        value = jnp.where(zone == level, table[level, column], value)
                    out[column, x] = value
                return carry

            lax.fori_loop(0, zone_ref.shape[0], step, 0)

    outs = [jax.ShapeDtypeStruct((7,) + z.shape, jnp.float32) for z in (zone_fine, zone_coarse)]
    return call(kernel, "materials", (table,), (zone_fine, zone_coarse), outs, [], 5 * 10**6)


def velocity_step(sizes, place, interp, restrict, halos, fields, props, velocity):
    def kernel(
        place, interp, restrict, latE, latO, depE, depO, diag, sf, sc, pf, pc, vf, vc,
        of, oc, latE2, latO2, depE2, depO2, diag2, xlo, xhi, zlo, zhi, lift, gather,
    ):
        receive(sizes, place, latE, latO, depE, depO, diag, STRESS_Z, interp, xlo, xhi, zlo, zhi, lift)
        fine = Grid(sizes, True, sf, STRESS_X, STRESS_Z, xlo, xhi, zlo, zhi)
        velocity_rows(fine, vf, of, pf)
        coarse = Grid(sizes, False, sc, STRESS_X, STRESS_Z, xlo, xhi, zlo, zhi)
        velocity_rows(coarse, vc, oc, pc)
        send(sizes, place, of, oc, VELOCITY_X, VELOCITY_Z, restrict, latE2, latO2, depE2, depO2, diag2, gather)

    outs = [like(v) for v in velocity] + packs(sizes)
    out = call(
        kernel, "velocity_step", (place, interp, restrict), (*halos, *fields, *props, *velocity), outs,
        halo_scratch(sizes) + [gather_scratch(sizes)], 10**7,
    )
    return out[:2], out[2:]


def stress_step(sizes, place, interp, restrict, halos, velocity, props, stress, memory, again):
    def kernel(
        place, interp, restrict, latE, latO, depE, depO, diag, vf, vc, pf, pc, sf, sc, mf, mc,
        osf, osc, omf, omc, *rest,
    ):
        outgoing, (xlo, xhi, zlo, zhi, lift, gather) = rest[:-6], rest[-6:]
        receive(sizes, place, latE, latO, depE, depO, diag, VELOCITY_Z, interp, xlo, xhi, zlo, zhi, lift)
        fine = Grid(sizes, True, vf, VELOCITY_X, VELOCITY_Z, xlo, xhi, zlo, zhi)
        stress_rows(fine, sf, mf, osf, omf, pf)
        coarse = Grid(sizes, False, vc, VELOCITY_X, VELOCITY_Z, xlo, xhi, zlo, zhi)
        stress_rows(coarse, sc, mc, osc, omc, pc)
        if again:
            send(sizes, place, osf, osc, STRESS_X, STRESS_Z, restrict, *outgoing, gather)

    outs = [like(x) for x in (*stress, *memory)] + (packs(sizes) if again else [])
    out = call(
        kernel, "stress_step", (place, interp, restrict), (*halos, *velocity, *props, *stress, *memory), outs,
        halo_scratch(sizes) + [gather_scratch(sizes)], 2 * 10**7,
    )
    return out[:2], out[2:4], out[4:]


def rotation(low, high, pivot):
    gap = high - low
    twice = pivot + pivot
    square = twice * twice
    length2 = jnp.maximum(gap * gap + square, TINY)
    length = length2 * lax.rsqrt(length2)
    signed = jnp.where(gap >= 0, length, -length)
    middle = 0.5 * (low + high)
    reach = 0.5 * signed
    base = gap + signed

    def turn():
        inverse = lax.rsqrt(base * base + square)
        return base * inverse, twice * inverse

    return middle - reach, middle + reach, turn


def largest_eigenvalue(a, b, c, ab, ac, bc):
    a, b, turn = rotation(a, b, ab)
    cosine, sine = turn()
    ac, bc = cosine * ac - sine * bc, sine * ac + cosine * bc
    for sweep in range(3):
        if sweep > 0:
            a, b, turn = rotation(a, b, ab)
            cosine, sine = turn()
            ac, bc = cosine * ac, sine * ac
        a, c, turn = rotation(a, c, ac)
        cosine, sine = turn()
        ab, bc = -(sine * bc), cosine * bc
        b, c, turn = rotation(b, c, bc)
        if sweep < 2:
            cosine, sine = turn()
            ab, ac = cosine * ab, sine * ab
    return jnp.maximum(jnp.maximum(a, b), c)


def peaks(stress, props, peak):
    def kernel(sf, sc, pf, pc, kf, kc, of, oc):
        for s, p, k, o in ((sf, pf, kf, of), (sc, pc, kc, oc)):

            def step(x, carry, s=s, p=p, k=k, o=o):
                xx, yy, zz = s[0, x], s[1, x], s[2, x]
                top = largest_eigenvalue(xx, yy, zz, s[3, x], s[4, x], s[5, x])
                principal = (top - p[ISO, x] * (xx + yy + zz)) * p[SCALE, x]
                o[x] = jnp.maximum(k[x], principal)
                return carry

            lax.fori_loop(0, s.shape[1], step, 0)

    return call(kernel, "peaks", (), (*stress, *props, *peak), [like(k) for k in peak], [], 4 * 10**7)


def exchanged(arrays):
    latE, latO, depE, depO, diag = arrays
    lat, depth = lax.axis_size("lat"), lax.axis_size("depth")

    def swaps(count, first):
        pairs = [(i, (i + 1) % count) for i in range(first, count, 2)]
        return pairs + [(b, a) for a, b in pairs]

    across = [((i + 1) * depth, i * depth + depth - 1) for i in range(lat - 1)]
    diag = lax.ppermute(diag, ("lat", "depth"), across)
    depO = lax.ppermute(depO, "depth", swaps(depth, 1))
    depE = lax.ppermute(depE, "depth", swaps(depth, 0))
    latO = lax.ppermute(latO, "lat", swaps(lat, 1))
    latE = lax.ppermute(latE, "lat", swaps(lat, 0))
    return (latE, latO, depE, depO, diag)


def on_device(
    velocity_fine,
    stress_fine,
    memory_fine,
    peak_fine,
    zone_fine,
    velocity_coarse,
    stress_coarse,
    memory_coarse,
    peak_coarse,
    zone_coarse,
    zone_table,
    interp_weight,
    restrict_weight,
):
    sizes = Sizes(stress_fine.shape[1:], stress_coarse.shape[1:])
    place = jnp.stack(
        [
            lax.axis_index("lat"),
            lax.axis_index("depth"),
            jnp.int32(lax.axis_size("lat")),
            jnp.int32(lax.axis_size("depth")),
        ]
    ).astype(jnp.int32)
    buoyancy, lame, shear, decay, damping = [zone_table[:, i] for i in range(5)]
    table = jnp.stack(
        [
            buoyancy,
            lame,
            2.0 * shear,
            decay,
            damping * (1.0 - decay),
            lame / (3.0 * lame + 2.0 * shear),
            0.5 / shear,
        ],
        axis=1,
    )
    velocity = (velocity_fine, velocity_coarse)
    stress = (stress_fine, stress_coarse)
    memory = (memory_fine, memory_coarse)
    peak = (peak_fine, peak_coarse)
    outgoing = pack_stress(sizes, place, restrict_weight, *stress)
    props = materials(table, zone_fine, zone_coarse)
    for step in range(STEPS):
        halos = exchanged(outgoing)
        if step > 0:
            peak = peaks(stress, props, peak)
        velocity, outgoing = velocity_step(
            sizes, place, interp_weight, restrict_weight, halos, stress, props, velocity
        )
        halos = exchanged(outgoing)
        stress, memory, outgoing = stress_step(
            sizes, place, interp_weight, restrict_weight, halos, velocity, props, stress, memory, step + 1 < STEPS
        )
    peak = peaks(stress, props, peak)
    return (velocity[0], stress[0], memory[0], peak[0], velocity[1], stress[1], memory[1], peak[1])


def solution(mesh):
    field = P(None, "lat", "depth", None)
    scalar = P("lat", "depth", None)
    grid = (field, field, field, scalar)
    return jax.shard_map(
        on_device,
        mesh=mesh,
        in_specs=(*grid, scalar, *grid, scalar, P(), P(), P()),
        out_specs=(*grid, *grid),
        check_vma=False,
    )
```

```python
import functools

import jax
import jax.numpy as jnp
from jax import lax
from jax.experimental import pallas as pl
from jax.experimental.pallas import tpu as pltpu
from jax.sharding import PartitionSpec as P

STEPS = 2
DT = 0.4
NEAR = 9.0 / 8.0
FAR = 1.0 / 24.0
TINY = 1e-36

STRESS_X = ([(0, 1), (3, 2), (3, 1), (4, 2), (4, 1)], [(0, 0), (0, 1), (3, 0), (4, 0)])
STRESS_Z = ([(4, 2), (4, 1), (5, 2), (5, 1), (2, 1)], [(4, 0), (5, 0), (2, 0), (2, 1)])
VELOCITY_X = ([(0, 2), (0, 1), (1, 1), (2, 1)], [(0, 0), (1, 0), (1, 1), (2, 0), (2, 1)])
VELOCITY_Z = ([(2, 2), (2, 1), (0, 1), (1, 1)], [(2, 0), (0, 0), (0, 1), (1, 0), (1, 1)])

BULK = 2 * 10**6
CB, LAME, MU2, DECAY, DAMP, ISO, SCALE = range(7)


class Sizes:
    def __init__(self, fine, coarse):
        self.lats, self.depths = lax.axis_size("lat"), lax.axis_size("depth")
        self.fx, self.fz, self.fy = fine
        self.cx, self.cz, self.cy = coarse
        self.lanes = self.fy // self.cy
        self.lat_fine = 5 * self.fz
        self.lat_rows = self.lat_fine + -(-5 // self.lanes) * self.cz
        self.dep_fine = 5 * self.fx
        used = self.dep_fine + 5 * -(-self.cx // self.lanes)
        self.dep_rows = -(-used // 8) * 8

    def lat_slot(self, k):
        row = self.lat_fine + (k // self.lanes) * self.cz
        lane = (k % self.lanes) * self.cy
        return (slice(row, row + self.cz), slice(lane, lane + self.cy))

    def dep_slot(self, k, x):
        row = self.dep_fine + (x // self.lanes) * 5 + k
        lane = (x % self.lanes) * self.cy
        return (slice(row, row + 1), slice(lane, lane + self.cy))


def y_shift(f, offset, lane):
    width = f.shape[1]
    moved = pltpu.roll(f, (-offset) % width, 1)
    inside = lane < width - offset if offset > 0 else lane >= -offset
    return jnp.where(inside, moved, 0.0)


def z_shift(f, offset, row):
    depth = f.shape[0]
    moved = pltpu.roll(f, (-offset) % depth, 0)
    inside = row < depth - offset if offset > 0 else row >= -offset
    return jnp.where(inside, moved, 0.0)


def parts(at, up):
    def minus(a, b):
        if a is None or b is None:
            return a if b is None else -b
        return a - b

    if up:
        return minus(at(1), at(0)), minus(at(2), at(-1))
    return minus(at(0), at(-1)), minus(at(1), at(-2))


class Grid:
    def __init__(self, field, spacing):
        self.field, self.spacing = field, spacing
        _, self.nx, self.nz, self.ny = field.shape
        self.row = lax.broadcasted_iota(jnp.int32, (self.nz, self.ny), 0)
        self.lane = lax.broadcasted_iota(jnp.int32, (self.nz, self.ny), 1)

    def dx(self, comp, x, up):
        def at(offset):
            if isinstance(x, int) and not 0 <= x + offset < self.nx:
                return None
            return self.field[comp, x + offset]

        return parts(at, up)

    def dy(self, comp, x, up):
        f = self.field[comp, x]
        return parts(lambda offset: y_shift(f, offset, self.lane) if offset else f, up)

    def dz(self, comp, x, up):
        f = self.field[comp, x]
        return parts(lambda offset: z_shift(f, offset, self.row) if offset else f, up)


def over_rows(count, body):
    if count <= 8:
        for x in range(count):
            body(x)
        return

    def step(x, carry):
        body(x)
        return carry

    for x in (0, 1):
        body(x)
    lax.fori_loop(2, count - 2, step, 0)
    for x in (count - 2, count - 1):
        body(x)


def combine(*pairs):
    near = [p[0] for p in pairs if p[0] is not None]
    far = [p[1] for p in pairs if p[1] is not None]
    return NEAR * functools.reduce(jnp.add, near) - FAR * functools.reduce(jnp.add, far)


def velocity_rows(grid, velocity, out, props):
    scale = DT / grid.spacing

    def body(x):
        speed = scale * props[CB, x]
        ax = combine(grid.dx(0, x, True), grid.dy(3, x, False), grid.dz(4, x, False))
        out[0, x] = velocity[0, x] + speed * ax
        ay = combine(grid.dx(3, x, False), grid.dy(1, x, True), grid.dz(5, x, False))
        out[1, x] = velocity[1, x] + speed * ay
        az = combine(grid.dx(4, x, False), grid.dy(5, x, False), grid.dz(2, x, True))
        out[2, x] = velocity[2, x] + speed * az

    over_rows(grid.nx, body)


def stress_rows(grid, stress, memory, stress_out, memory_out, props):
    inverse = 1.0 / grid.spacing

    def body(x):
        lame, twice = props[LAME, x], props[MU2, x]
        decay, damp = props[DECAY, x], props[DAMP, x]
        if inverse != 1.0:
            lame, twice = lame * inverse, twice * inverse
        half = 0.5 * twice

        def finish(comp, rate):
            old = memory[comp, x]
            new = decay * old - damp * rate
            memory_out[comp, x] = new
            stress_out[comp, x] = stress[comp, x] + DT * (rate + 0.5 * (old + new))

        xx = combine(grid.dx(0, x, False))
        yy = combine(grid.dy(1, x, False))
        zz = combine(grid.dz(2, x, False))
        volume = lame * (xx + yy + zz)
        finish(0, volume + twice * xx)
        finish(1, volume + twice * yy)
        finish(2, volume + twice * zz)
        finish(3, half * combine(grid.dy(0, x, True), grid.dx(1, x, True)))
        finish(4, half * combine(grid.dz(0, x, True), grid.dx(2, x, True)))
        finish(5, half * combine(grid.dz(1, x, True), grid.dy(2, x, True)))

    over_rows(grid.nx, body)


class Edges:
    def __init__(self, sizes, fine, x_lists, z_lists, halo):
        self.sizes, self.fine = sizes, fine
        self.x_lists, self.z_lists = x_lists, z_lists
        self.xlo, self.xhi, self.zlo, self.zhi = halo
        self.nx, self.nz, self.ny = (
            (sizes.fx, sizes.fz, sizes.fy) if fine else (sizes.cx, sizes.cz, sizes.cy)
        )
        self.spacing = 1.0 if fine else 3.0
        self.row = lax.broadcasted_iota(jnp.int32, (8, self.ny), 0)

    def x_layer(self, ref, k):
        if self.fine:
            return ref[k * self.nz : (k + 1) * self.nz, :]
        return ref[self.sizes.lat_slot(k)]

    def low_x(self, comp, r):
        return self.x_layer(self.xlo, self.x_lists[0].index((comp, r)))

    def high_x(self, comp, r):
        return self.x_layer(self.xhi, self.x_lists[1].index((comp, r)))

    def dx(self, comp, x, up):
        if not isinstance(x, int):
            return None
        back = x - (self.nx - 1)
        if up:
            terms = {0: lambda: FAR * self.low_x(comp, 1)}
            ends = {
                0: lambda: NEAR * self.high_x(comp, 0) - FAR * self.high_x(comp, 1),
                -1: lambda: -FAR * self.high_x(comp, 0),
            }
        else:
            terms = {
                0: lambda: FAR * self.low_x(comp, 2) - NEAR * self.low_x(comp, 1),
                1: lambda: FAR * self.low_x(comp, 1),
            }
            ends = {0: lambda: -FAR * self.high_x(comp, 0)}
        found = [f() for f in (terms.get(x), ends.get(back)) if f is not None]
        return functools.reduce(jnp.add, found) if found else None

    def z_row(self, ref, k, x):
        if not self.fine:
            return ref[self.sizes.dep_slot(k, x)]
        if isinstance(x, int):
            return ref[k * self.nx + x : k * self.nx + x + 1, :]
        return ref[pl.ds(k * self.nx + x, 1), :]

    def dz(self, comp, x, up):
        low = {r: self.z_row(self.zlo, k, x) for k, (c, r) in enumerate(self.z_lists[0]) if c == comp}
        high = {r: self.z_row(self.zhi, k, x) for k, (c, r) in enumerate(self.z_lists[1]) if c == comp}
        row = self.row
        if up:
            top = jnp.where(row == 0, FAR * low[1], 0.0)
            bottom = jnp.where(
                row == 7, NEAR * high[0] - FAR * high[1], jnp.where(row == 6, -FAR * high[0], 0.0)
            )
        else:
            top = jnp.where(row == 0, FAR * low[2] - NEAR * low[1], jnp.where(row == 1, FAR * low[1], 0.0))
            bottom = jnp.where(row == 7, -FAR * high[0], 0.0)
        middle = [jnp.zeros((self.nz - 16, self.ny), jnp.float32)] if self.nz > 16 else []
        return jnp.concatenate([top, *middle, bottom], axis=0)


def total(*terms):
    found = [t for t in terms if t is not None]
    return functools.reduce(jnp.add, found) if found else None


def velocity_edges(edges, velocity, out, props):
    scale = DT / edges.spacing

    def body(x):
        speed = scale * props[CB, x]
        for comp, across, back, down, up in ((0, 0, True, 4, False), (1, 3, False, 5, False), (2, 4, False, 2, True)):
            added = total(edges.dx(across, x, back), edges.dz(down, x, up))
            out[comp, x] = velocity[comp, x] + speed * added

    over_rows(edges.nx, body)


def stress_edges(edges, stress, memory, stress_out, memory_out, props, then=None):
    inverse = 1.0 / edges.spacing

    def body(x):
        damp = props[DAMP, x]
        gain = DT - (0.5 * DT) * damp
        twice = inverse * props[MU2, x]
        half = 0.5 * twice

        def put(comp, rate):
            memory_out[comp, x] = memory[comp, x] if rate is None else memory[comp, x] - damp * rate
            stress_out[comp, x] = stress[comp, x] if rate is None else stress[comp, x] + gain * rate

        xx, zz = edges.dx(0, x, False), edges.dz(2, x, False)
        volume = inverse * props[LAME, x] * total(xx, zz)
        put(0, volume if xx is None else volume + twice * xx)
        put(1, volume)
        put(2, volume + twice * zz)
        xy = edges.dx(1, x, True)
        put(3, None if xy is None else half * xy)
        put(4, half * total(edges.dx(2, x, True), edges.dz(0, x, True)))
        put(5, half * edges.dz(1, x, True))
        if then is not None:
            then(x)

    over_rows(edges.nx, body)


def receive(sizes, halos, z_lists, interp, halo, lift):
    depO, diag, depE, latO, latE = halos
    xlo, xhi, zlo, zhi = halo
    lat, depth = lax.axis_index("lat"), lax.axis_index("depth")
    lat_even, depth_even = lax.rem(lat, 2) == 0, lax.rem(depth, 2) == 0
    last_lat, last_depth = sizes.lats - 1, sizes.depths - 1

    @pl.when(lat_even)
    def _():
        xlo[...] = latO[...]
        xhi[...] = latE[...]

    @pl.when(jnp.logical_not(lat_even))
    def _():
        xlo[...] = latE[...]
        xhi[...] = latO[...]

    @pl.when(lat == 0)
    def _():
        xlo[...] = jnp.zeros_like(xlo)

    @pl.when(lat == last_lat)
    def _():
        xhi[...] = jnp.zeros_like(xhi)

    @pl.when(depth_even)
    def _():
        zlo[...] = depO[...]
        zhi[...] = depE[...]

    @pl.when(jnp.logical_not(depth_even))
    def _():
        zlo[...] = depE[...]
        zhi[...] = depO[...]

    @pl.when(depth == 0)
    def _():
        zlo[0 : sizes.dep_fine, :] = jnp.zeros((sizes.dep_fine, sizes.fy), jnp.float32)

    @pl.when(depth == last_depth)
    def _():
        count = len(z_lists[1])
        lift[...] = jnp.zeros_like(lift)
        beyond = jnp.where(lat == last_lat, 0.0, 1.0)
        for k in range(count):
            planes = [depO[sizes.dep_slot(k, a)] for a in range(sizes.cx)]
            planes.append(diag[k : k + 1, :] * beyond)
            for a in range(sizes.cx):
                for p in range(3):
                    share = interp[0, p].astype(jnp.float32) * 0.125
                    x = k * sizes.fx + 3 * a + p
                    lift[x : x + 1, :] = share * planes[a] + (1.0 - share) * planes[a + 1]
        c = lax.broadcasted_iota(jnp.int32, (sizes.cy, sizes.fy), 0)
        f = lax.broadcasted_iota(jnp.int32, (sizes.cy, sizes.fy), 1)
        gap = f - 3 * c
        spread = jnp.zeros((sizes.cy, sizes.fy), jnp.float32)
        for p in range(3):
            share = interp[1, p].astype(jnp.float32) * 0.125
            spread = jnp.where(gap == p, share, spread)
            spread = jnp.where(gap == p - 3, 1.0 - share, spread)
        ghost = jnp.dot(
            lift[...], spread, precision=lax.Precision.HIGHEST, preferred_element_type=jnp.float32
        )
        zhi[...] = jnp.zeros_like(zhi)
        zhi[0 : sizes.dep_fine, :] = ghost[0 : sizes.dep_fine, :]


def send(sizes, fine, coarse, x_lists, z_lists, restrict, buffers, gather):
    depO, diag, depE, latO, latE = buffers
    lat, depth = lax.axis_index("lat"), lax.axis_index("depth")
    lat_even, depth_even = lax.rem(lat, 2) == 0, lax.rem(depth, 2) == 0
    last_depth = sizes.depths - 1

    def pack_x(up, down):
        for ref, entries, high in ((up, x_lists[0], True), (down, x_lists[1], False)):
            for k, (comp, r) in enumerate(entries):
                ref[k * sizes.fz : (k + 1) * sizes.fz, :] = fine[comp, sizes.fx - r if high else r]
                ref[sizes.lat_slot(k)] = coarse[comp, sizes.cx - r if high else r]

    def pack_z(up, down):
        for ref, entries, high in ((up, z_lists[0], True), (down, z_lists[1], False)):
            for k, (comp, r) in enumerate(entries):
                z = sizes.fz - r if high else r
                for x in range(sizes.fx):
                    ref[k * sizes.fx + x : k * sizes.fx + x + 1, :] = fine[comp, x, z : z + 1, :]
                z = sizes.cz - r if high else r
                for x in range(sizes.cx):
                    ref[sizes.dep_slot(k, x)] = coarse[comp, x, z : z + 1, :]

    @pl.when(lat_even)
    def _():
        pack_x(latE, latO)

    @pl.when(jnp.logical_not(lat_even))
    def _():
        pack_x(latO, latE)

    @pl.when(depth_even)
    def _():
        pack_z(depE, depO)

    @pl.when(jnp.logical_not(depth_even))
    def _():
        pack_z(depO, depE)

    diag[...] = jnp.zeros_like(diag)

    @pl.when(depth == 0)
    def _():
        for k, (comp, j) in enumerate(z_lists[1]):
            for x in range(sizes.cx):
                plane = ((2.0 - j) * coarse[comp, x, 0:1, :] + (1.0 + j) * coarse[comp, x, 1:2, :]) / 3.0
                depO[sizes.dep_slot(k, x)] = plane
                if x == 0:
                    diag[k : k + 1, :] = plane

    @pl.when(depth == last_depth)
    def _():
        wx = [restrict[0, p].astype(jnp.float32) for p in range(3)]
        wy = [restrict[1, p].astype(jnp.float32) for p in range(3)]
        gather[...] = jnp.zeros_like(gather)
        for k, (comp, r) in enumerate(z_lists[0]):
            z = sizes.fz - 3 * r
            for a in range(sizes.cx):
                total = None
                for p in range(3):
                    f = fine[comp, 3 * a + p, z : z + 3, :]
                    layers = wx[p] * (f[0:1] + f[1:2] + f[2:3])
                    total = layers if total is None else total + layers
                row = k * sizes.cx + a
                gather[row : row + 1, :] = total
        f = lax.broadcasted_iota(jnp.int32, (sizes.fy, sizes.cy), 0)
        c = lax.broadcasted_iota(jnp.int32, (sizes.fy, sizes.cy), 1)
        gap = f - 3 * c
        table = jnp.zeros((sizes.fy, sizes.cy), jnp.float32)
        for p in range(3):
            table = jnp.where(gap == p, wy[p], table)
        summed = jnp.dot(
            gather[...], table, precision=lax.Precision.HIGHEST, preferred_element_type=jnp.float32
        )
        norm = jnp.full((1, sizes.cy), 3.0 * (wx[0] + wx[1] + wx[2]) * (wy[0] + wy[1] + wy[2]))
        lifted = summed / norm
        for k in range(len(z_lists[0])):
            for a in range(sizes.cx):
                row = k * sizes.cx + a
                depO[sizes.dep_slot(k, a)] = lifted[row : row + 1, :]


SMEM = pl.BlockSpec(memory_space=pltpu.SMEM)
VMEM = pl.BlockSpec(memory_space=pltpu.VMEM)
HBM = pl.BlockSpec(memory_space=pltpu.HBM)
LIMIT = 24 * 1024 * 1024
PACK_LIMIT = 63 * 1024 * 1024
FIRST_LIMIT = 40 * 1024 * 1024


def packs(sizes):
    lat = jax.ShapeDtypeStruct((sizes.lat_rows, sizes.fy), jnp.float32)
    dep = jax.ShapeDtypeStruct((sizes.dep_rows, sizes.fy), jnp.float32)
    return [dep, jax.ShapeDtypeStruct((8, sizes.cy), jnp.float32), dep, lat, lat]


def halo_scratch(sizes):
    lat = pltpu.VMEM((sizes.lat_rows, sizes.fy), jnp.float32)
    dep = pltpu.VMEM((sizes.dep_rows, sizes.fy), jnp.float32)
    return [lat, lat, dep, dep, pltpu.VMEM((-(-sizes.dep_fine // 8) * 8, sizes.cy), jnp.float32)]


def gather_scratch(sizes):
    return pltpu.VMEM((-(-5 * sizes.cx // 8) * 8, sizes.fy), jnp.float32)


def like(x):
    return jax.ShapeDtypeStruct(x.shape, x.dtype)


def call(kernel, name, smem, vmem, outs, scratch, work, far=(), far_outs=(), limit=LIMIT):
    outs = [*far_outs, *outs]
    moved = sum(x.size * 4 for x in (*far, *vmem)) + sum(4 * o.size for o in outs)
    return pl.pallas_call(
        kernel,
        name=name,
        out_shape=outs,
        in_specs=[SMEM] * len(smem) + [HBM] * len(far) + [VMEM] * len(vmem),
        out_specs=[HBM] * len(far_outs) + [VMEM] * (len(outs) - len(far_outs)),
        scratch_shapes=scratch,
        compiler_params=pltpu.CompilerParams(vmem_limit_bytes=limit),
        cost_estimate=pl.CostEstimate(flops=work, bytes_accessed=moved, transcendentals=0),
    )(*smem, *far, *vmem)


def room(x):
    return pltpu.VMEM(x.shape, x.dtype)


def pack_stress(sizes, restrict, fine, coarse):
    def kernel(restrict, fine, coarse, *rest):
        buffers, (gather, near_fine, near_coarse, sems) = rest[:5], rest[5:]
        fx = sizes.fx
        copies = []
        for source, target, part in (
            (fine, near_fine, (slice(4, 6),)),
            (fine, near_fine, (2,)),
            (coarse, near_coarse, (slice(2, 6),)),
            (coarse, near_coarse, (0,)),
            (fine, near_fine, (0, slice(0, 2))),
            (fine, near_fine, (0, slice(fx - 1, fx))),
            (fine, near_fine, (3, slice(0, 1))),
            (fine, near_fine, (3, slice(fx - 2, fx))),
        ):
            copies.append(pltpu.make_async_copy(source.at[part], target.at[part], sems.at[len(copies)]))
        for copy in copies:
            copy.start()
        for copy in copies:
            copy.wait()
        send(sizes, near_fine, near_coarse, STRESS_X, STRESS_Z, restrict, buffers, gather)

    scratch = [gather_scratch(sizes), room(fine), room(coarse), pltpu.SemaphoreType.DMA((8,))]
    return call(
        kernel, "pack_stress", (restrict,), (), packs(sizes), scratch, 10**6, far=(fine, coarse), limit=PACK_LIMIT
    )


def material_rows(table, zone, out):
    def step(x, carry):
        kind = zone[x]
        for column in range(7):
            value = jnp.full(kind.shape, table[7, column])
            for level in range(7):
                value = jnp.where(kind == level, table[level, column], value)
            out[column, x] = value
        return carry

    lax.fori_loop(0, zone.shape[0], step, 0)


def first_bulk(table, zones, stress, velocity):
    def kernel(table, *rest):
        far, (of, oc, pf, pc), near, sems = rest[:6], rest[6:10], rest[10:16], rest[16]
        copies = [pltpu.make_async_copy(a, b, sems.at[i]) for i, (a, b) in enumerate(zip(far, near))]
        for copy in copies:
            copy.start()
        zf, zc, sf, sc, vf, vc = near
        copies[0].wait()
        material_rows(table, zf, pf)
        copies[1].wait()
        material_rows(table, zc, pc)
        for copy in copies[2:]:
            copy.wait()
        velocity_rows(Grid(sf, 1.0), vf, of, pf)
        velocity_rows(Grid(sc, 3.0), vc, oc, pc)

    outs = [like(v) for v in velocity]
    outs += [jax.ShapeDtypeStruct((7,) + z.shape, jnp.float32) for z in zones]
    far = (*zones, *stress, *velocity)
    scratch = [room(x) for x in far] + [pltpu.SemaphoreType.DMA((6,))]
    out = call(kernel, "first_bulk", (table,), (), outs, scratch, BULK, far=far, limit=FIRST_LIMIT)
    return out[:2], out[2:]


def velocity_bulk(stress, props, velocity, peak):
    def kernel(sf, sc, pf, pc, vf, vc, *rest):
        kf, kc, of, oc, okf, okc = rest
        velocity_rows(Grid(sf, 1.0), vf, of, pf)
        velocity_rows(Grid(sc, 3.0), vc, oc, pc)
        peak_rows(sf, pf, kf, okf)
        peak_rows(sc, pc, kc, okc)

    outs = [like(x) for x in (*velocity, *peak)]
    out = call(kernel, "velocity_bulk", (), (*stress, *props, *velocity, *peak), outs, [], BULK)
    return out[:2], out[2:]


def stress_bulk(velocity, props, stress, memory):
    def kernel(vf, vc, pf, pc, sf, sc, mf, mc, osf, osc, omf, omc):
        stress_rows(Grid(vf, 1.0), sf, mf, osf, omf, pf)
        stress_rows(Grid(vc, 3.0), sc, mc, osc, omc, pc)

    outs = [like(x) for x in (*stress, *memory)]
    return call(kernel, "stress_bulk", (), (*velocity, *props, *stress, *memory), outs, [], BULK)


def velocity_finish(sizes, interp, restrict, halos, props, velocity):
    def kernel(interp, restrict, *rest):
        halos, (pf, pc), (vf, vc), (of, oc), buffers = rest[:5], rest[5:7], rest[7:9], rest[9:11], rest[11:16]
        halo, (lift, gather) = rest[16:20], rest[20:]
        receive(sizes, halos, STRESS_Z, interp, halo, lift)
        velocity_edges(Edges(sizes, True, STRESS_X, STRESS_Z, halo), vf, of, pf)
        velocity_edges(Edges(sizes, False, STRESS_X, STRESS_Z, halo), vc, oc, pc)
        send(sizes, of, oc, VELOCITY_X, VELOCITY_Z, restrict, buffers, gather)

    outs = [like(v) for v in velocity] + packs(sizes)
    out = call(
        kernel, "velocity_finish", (interp, restrict), (*halos, *props, *velocity), outs,
        halo_scratch(sizes) + [gather_scratch(sizes)], 10**7,
    )
    return out[:2], out[2:]


def stress_finish(sizes, interp, restrict, halos, props, stress, memory):
    def kernel(interp, restrict, *rest):
        halos, (pf, pc), (sf, sc, mf, mc), (osf, osc, omf, omc) = rest[:5], rest[5:7], rest[7:11], rest[11:15]
        outgoing, halo, (lift, gather) = rest[15:20], rest[20:24], rest[24:]
        receive(sizes, halos, VELOCITY_Z, interp, halo, lift)
        stress_edges(Edges(sizes, True, VELOCITY_X, VELOCITY_Z, halo), sf, mf, osf, omf, pf)
        stress_edges(Edges(sizes, False, VELOCITY_X, VELOCITY_Z, halo), sc, mc, osc, omc, pc)
        send(sizes, osf, osc, STRESS_X, STRESS_Z, restrict, outgoing, gather)

    outs = [like(x) for x in (*stress, *memory)] + packs(sizes)
    out = call(
        kernel, "stress_finish", (interp, restrict), (*halos, *props, *stress, *memory), outs,
        halo_scratch(sizes) + [gather_scratch(sizes)], 2 * 10**7,
    )
    return out[:2], out[2:4], out[4:]


def last_finish(sizes, interp, halos, props, stress, memory, peak, velocity):
    def kernel(interp, *rest):
        halos, (pf, pc), (sf, sc, mf, mc), (kf, kc), speeds = rest[:5], rest[5:7], rest[7:11], rest[11:13], rest[13:15]
        outs, halo, lift = rest[15:23], rest[23:27], rest[27]
        near, sems = rest[28:34], rest[34]

        def whole(i):
            source = speeds[i] if i < 2 else near[i - 2]
            return pltpu.make_async_copy(source, outs[i], sems.at[i])

        for i in range(2):
            whole(i).start()
        receive(sizes, halos, VELOCITY_Z, interp, halo, lift)
        osf, osc, omf, omc, okf, okc = near

        def store(x):
            for i in (2, 4):
                pltpu.make_async_copy(near[i - 2].at[:, x], outs[i].at[:, x], sems.at[i]).start()

        stress_edges(Edges(sizes, True, VELOCITY_X, VELOCITY_Z, halo), sf, mf, osf, omf, pf, store)
        stress_edges(Edges(sizes, False, VELOCITY_X, VELOCITY_Z, halo), sc, mc, osc, omc, pc)
        for i in (3, 5):
            whole(i).start()
        peak_rows(osf, pf, kf, okf)
        whole(6).start()
        peak_rows(osc, pc, kc, okc)
        whole(7).start()
        for i in range(8):
            whole(i).wait()

    outs = [like(x) for x in (*velocity, *stress, *memory, *peak)]
    scratch = halo_scratch(sizes) + [room(x) for x in (*stress, *memory, *peak)] + [pltpu.SemaphoreType.DMA((8,))]
    out = call(
        kernel, "last_finish", (interp,), (*halos, *props, *stress, *memory, *peak, *velocity), [],
        scratch, 2 * 10**7, far_outs=outs,
    )
    return out[:2], out[2:4], out[4:6], out[6:]


def rotation(low, high, pivot):
    gap = high - low
    twice = pivot + pivot
    square = twice * twice
    length2 = jnp.maximum(gap * gap + square, TINY)
    length = length2 * lax.rsqrt(length2)
    signed = jnp.where(gap >= 0, length, -length)
    middle = 0.5 * (low + high)
    reach = 0.5 * signed
    base = gap + signed

    def turn():
        inverse = lax.rsqrt(base * base + square)
        return base * inverse, twice * inverse

    return middle - reach, middle + reach, turn


def largest_eigenvalue(a, b, c, ab, ac, bc):
    a, b, turn = rotation(a, b, ab)
    cosine, sine = turn()
    ac, bc = cosine * ac - sine * bc, sine * ac + cosine * bc
    for sweep in range(3):
        if sweep > 0:
            a, b, turn = rotation(a, b, ab)
            cosine, sine = turn()
            ac, bc = cosine * ac, sine * ac
        a, c, turn = rotation(a, c, ac)
        cosine, sine = turn()
        ab, bc = -(sine * bc), cosine * bc
        b, c, turn = rotation(b, c, bc)
        if sweep < 2:
            cosine, sine = turn()
            ab, ac = cosine * ab, sine * ab
    return jnp.maximum(jnp.maximum(a, b), c)


def peak_rows(stress, props, peak, out, width=2):
    def step(i, carry):
        x = pl.ds(i * width, width)
        xx, yy, zz, xy, xz, yz = [stress[comp, x] for comp in range(6)]
        top = largest_eigenvalue(xx, yy, zz, xy, xz, yz)
        principal = (top - props[ISO, x] * (xx + yy + zz)) * props[SCALE, x]
        out[x] = jnp.maximum(peak[x], principal)
        return carry

    lax.fori_loop(0, stress.shape[1] // width, step, 0)


def exchanged(arrays):
    depO, diag, depE, latO, latE = arrays
    lat, depth = lax.axis_size("lat"), lax.axis_size("depth")

    def swaps(count, first):
        pairs = [(i, (i + 1) % count) for i in range(first, count, 2)]
        return pairs + [(b, a) for a, b in pairs]

    across = [((i + 1) * depth, i * depth + depth - 1) for i in range(lat - 1)]
    depO = lax.ppermute(depO, "depth", swaps(depth, 1))
    diag = lax.ppermute(diag, ("lat", "depth"), across)
    depE = lax.ppermute(depE, "depth", swaps(depth, 0))
    latO = lax.ppermute(latO, "lat", swaps(lat, 1))
    latE = lax.ppermute(latE, "lat", swaps(lat, 0))
    return (depO, diag, depE, latO, latE)


def on_device(
    velocity_fine,
    stress_fine,
    memory_fine,
    peak_fine,
    zone_fine,
    velocity_coarse,
    stress_coarse,
    memory_coarse,
    peak_coarse,
    zone_coarse,
    zone_table,
    interp_weight,
    restrict_weight,
):
    sizes = Sizes(stress_fine.shape[1:], stress_coarse.shape[1:])
    buoyancy, lame, shear, decay, damping = [zone_table[:, i] for i in range(5)]
    table = jnp.stack(
        [
            buoyancy,
            lame,
            2.0 * shear,
            decay,
            damping * (1.0 - decay),
            lame / (3.0 * lame + 2.0 * shear),
            0.5 / shear,
        ],
        axis=1,
    )
    velocity = (velocity_fine, velocity_coarse)
    stress = (stress_fine, stress_coarse)
    memory = (memory_fine, memory_coarse)
    peak = (peak_fine, peak_coarse)
    outgoing = pack_stress(sizes, restrict_weight, *stress)
    for step in range(STEPS):
        halos = exchanged(outgoing)
        if step == 0:
            velocity, props = first_bulk(table, (zone_fine, zone_coarse), stress, velocity)
        else:
            velocity, peak = velocity_bulk(stress, props, velocity, peak)
        velocity, outgoing = velocity_finish(
            sizes, interp_weight, restrict_weight, halos, props, velocity
        )
        halos = exchanged(outgoing)
        bulk = stress_bulk(velocity, props, stress, memory)
        if step + 1 < STEPS:
            stress, memory, outgoing = stress_finish(
                sizes, interp_weight, restrict_weight, halos, props, bulk[:2], bulk[2:]
            )
        else:
            velocity, stress, memory, peak = last_finish(
                sizes, interp_weight, halos, props, bulk[:2], bulk[2:], peak, velocity
            )
    return (velocity[0], stress[0], memory[0], peak[0], velocity[1], stress[1], memory[1], peak[1])


def solution(mesh):
    field = P(None, "lat", "depth", None)
    scalar = P("lat", "depth", None)
    grid = (field, field, field, scalar)
    return jax.shard_map(
        on_device,
        mesh=mesh,
        in_specs=(*grid, scalar, *grid, scalar, P(), P(), P()),
        out_specs=(*grid, *grid),
        check_vma=False,
    )
```

```python
import functools

import jax
import jax.numpy as jnp
from jax import lax
from jax.experimental import pallas as pl
from jax.experimental.pallas import tpu as pltpu
from jax.sharding import PartitionSpec as P

STEPS = 2
DT = 0.4
NEAR = 9.0 / 8.0
FAR = 1.0 / 24.0
TINY = 1e-36

STRESS_X = ([(0, 1), (3, 2), (3, 1), (4, 2), (4, 1)], [(0, 0), (0, 1), (3, 0), (4, 0)])
STRESS_Z = ([(4, 2), (4, 1), (5, 2), (5, 1), (2, 1)], [(4, 0), (5, 0), (2, 0), (2, 1)])
VELOCITY_X = ([(0, 2), (0, 1), (1, 1), (2, 1)], [(0, 0), (1, 0), (1, 1), (2, 0), (2, 1)])
VELOCITY_Z = ([(2, 2), (2, 1), (0, 1), (1, 1)], [(2, 0), (0, 0), (0, 1), (1, 0), (1, 1)])

BULK = 2 * 10**6
CB, LAME, MU2, DECAY, DAMP, ISO, SCALE = range(7)


class Sizes:
    def __init__(self, fine, coarse):
        self.lats, self.depths = lax.axis_size("lat"), lax.axis_size("depth")
        self.fx, self.fz, self.fy = fine
        self.cx, self.cz, self.cy = coarse
        self.lanes = self.fy // self.cy
        self.lat_fine = 5 * self.fz
        self.lat_rows = self.lat_fine + -(-5 // self.lanes) * self.cz
        self.dep_fine = 5 * self.fx
        used = self.dep_fine + 5 * -(-self.cx // self.lanes)
        self.dep_rows = -(-used // 8) * 8

    def lat_slot(self, k):
        row = self.lat_fine + (k // self.lanes) * self.cz
        lane = (k % self.lanes) * self.cy
        return (slice(row, row + self.cz), slice(lane, lane + self.cy))

    def dep_slot(self, k, x):
        row = self.dep_fine + (x // self.lanes) * 5 + k
        lane = (x % self.lanes) * self.cy
        return (slice(row, row + 1), slice(lane, lane + self.cy))


def y_shift(f, offset, lane):
    width = f.shape[1]
    moved = pltpu.roll(f, (-offset) % width, 1)
    inside = lane < width - offset if offset > 0 else lane >= -offset
    return jnp.where(inside, moved, 0.0)


def z_shift(f, offset, row):
    depth = f.shape[0]
    moved = pltpu.roll(f, (-offset) % depth, 0)
    inside = row < depth - offset if offset > 0 else row >= -offset
    return jnp.where(inside, moved, 0.0)


def parts(at, up):
    def minus(a, b):
        if a is None or b is None:
            return a if b is None else -b
        return a - b

    if up:
        return minus(at(1), at(0)), minus(at(2), at(-1))
    return minus(at(0), at(-1)), minus(at(1), at(-2))


class Grid:
    def __init__(self, field, spacing):
        self.field, self.spacing = field, spacing
        _, self.nx, self.nz, self.ny = field.shape
        self.row = lax.broadcasted_iota(jnp.int32, (self.nz, self.ny), 0)
        self.lane = lax.broadcasted_iota(jnp.int32, (self.nz, self.ny), 1)

    def dx(self, comp, x, up):
        def at(offset):
            if isinstance(x, int) and not 0 <= x + offset < self.nx:
                return None
            return self.field[comp, x + offset]

        return parts(at, up)

    def dy(self, comp, x, up):
        f = self.field[comp, x]
        return parts(lambda offset: y_shift(f, offset, self.lane) if offset else f, up)

    def dz(self, comp, x, up):
        f = self.field[comp, x]
        return parts(lambda offset: z_shift(f, offset, self.row) if offset else f, up)


def over_rows(count, body):
    if count <= 8:
        for x in range(count):
            body(x)
        return

    def step(x, carry):
        body(x)
        return carry

    for x in (0, 1):
        body(x)
    lax.fori_loop(2, count - 2, step, 0)
    for x in (count - 2, count - 1):
        body(x)


def combine(*pairs):
    near = [p[0] for p in pairs if p[0] is not None]
    far = [p[1] for p in pairs if p[1] is not None]
    return NEAR * functools.reduce(jnp.add, near) - FAR * functools.reduce(jnp.add, far)


def velocity_rows(grid, velocity, out, props):
    scale = DT / grid.spacing

    def body(x):
        speed = scale * props[CB, x]
        ax = combine(grid.dx(0, x, True), grid.dy(3, x, False), grid.dz(4, x, False))
        out[0, x] = velocity[0, x] + speed * ax
        ay = combine(grid.dx(3, x, False), grid.dy(1, x, True), grid.dz(5, x, False))
        out[1, x] = velocity[1, x] + speed * ay
        az = combine(grid.dx(4, x, False), grid.dy(5, x, False), grid.dz(2, x, True))
        out[2, x] = velocity[2, x] + speed * az

    over_rows(grid.nx, body)


def stress_rows(grid, stress, memory, stress_out, memory_out, props):
    inverse = 1.0 / grid.spacing

    def body(x):
        lame, twice = props[LAME, x], props[MU2, x]
        decay, damp = props[DECAY, x], props[DAMP, x]
        if inverse != 1.0:
            lame, twice = lame * inverse, twice * inverse
        half = 0.5 * twice

        def finish(comp, rate):
            old = memory[comp, x]
            new = decay * old - damp * rate
            memory_out[comp, x] = new
            stress_out[comp, x] = stress[comp, x] + DT * (rate + 0.5 * (old + new))

        xx = combine(grid.dx(0, x, False))
        yy = combine(grid.dy(1, x, False))
        zz = combine(grid.dz(2, x, False))
        volume = lame * (xx + yy + zz)
        finish(0, volume + twice * xx)
        finish(1, volume + twice * yy)
        finish(2, volume + twice * zz)
        finish(3, half * combine(grid.dy(0, x, True), grid.dx(1, x, True)))
        finish(4, half * combine(grid.dz(0, x, True), grid.dx(2, x, True)))
        finish(5, half * combine(grid.dz(1, x, True), grid.dy(2, x, True)))

    over_rows(grid.nx, body)


class Edges:
    def __init__(self, sizes, fine, x_lists, z_lists, halo):
        self.sizes, self.fine = sizes, fine
        self.x_lists, self.z_lists = x_lists, z_lists
        self.xlo, self.xhi, self.zlo, self.zhi = halo
        self.nx, self.nz, self.ny = (
            (sizes.fx, sizes.fz, sizes.fy) if fine else (sizes.cx, sizes.cz, sizes.cy)
        )
        self.spacing = 1.0 if fine else 3.0
        self.row = lax.broadcasted_iota(jnp.int32, (8, self.ny), 0)

    def x_layer(self, ref, k):
        if self.fine:
            return ref[k * self.nz : (k + 1) * self.nz, :]
        return ref[self.sizes.lat_slot(k)]

    def low_x(self, comp, r):
        return self.x_layer(self.xlo, self.x_lists[0].index((comp, r)))

    def high_x(self, comp, r):
        return self.x_layer(self.xhi, self.x_lists[1].index((comp, r)))

    def dx(self, comp, x, up):
        if not isinstance(x, int):
            return None
        back = x - (self.nx - 1)
        if up:
            terms = {0: lambda: FAR * self.low_x(comp, 1)}
            ends = {
                0: lambda: NEAR * self.high_x(comp, 0) - FAR * self.high_x(comp, 1),
                -1: lambda: -FAR * self.high_x(comp, 0),
            }
        else:
            terms = {
                0: lambda: FAR * self.low_x(comp, 2) - NEAR * self.low_x(comp, 1),
                1: lambda: FAR * self.low_x(comp, 1),
            }
            ends = {0: lambda: -FAR * self.high_x(comp, 0)}
        found = [f() for f in (terms.get(x), ends.get(back)) if f is not None]
        return functools.reduce(jnp.add, found) if found else None

    def z_row(self, ref, k, x):
        if not self.fine:
            return ref[self.sizes.dep_slot(k, x)]
        if isinstance(x, int):
            return ref[k * self.nx + x : k * self.nx + x + 1, :]
        return ref[pl.ds(k * self.nx + x, 1), :]

    def dz(self, comp, x, up):
        low = {r: self.z_row(self.zlo, k, x) for k, (c, r) in enumerate(self.z_lists[0]) if c == comp}
        high = {r: self.z_row(self.zhi, k, x) for k, (c, r) in enumerate(self.z_lists[1]) if c == comp}
        row = self.row
        if up:
            top = jnp.where(row == 0, FAR * low[1], 0.0)
            bottom = jnp.where(
                row == 7, NEAR * high[0] - FAR * high[1], jnp.where(row == 6, -FAR * high[0], 0.0)
            )
        else:
            top = jnp.where(row == 0, FAR * low[2] - NEAR * low[1], jnp.where(row == 1, FAR * low[1], 0.0))
            bottom = jnp.where(row == 7, -FAR * high[0], 0.0)
        middle = [jnp.zeros((self.nz - 16, self.ny), jnp.float32)] if self.nz > 16 else []
        return jnp.concatenate([top, *middle, bottom], axis=0)


def total(*terms):
    found = [t for t in terms if t is not None]
    return functools.reduce(jnp.add, found) if found else None


def velocity_edges(edges, velocity, out, props):
    scale = DT / edges.spacing

    def body(x):
        speed = scale * props[CB, x]
        for comp, across, back, down, up in ((0, 0, True, 4, False), (1, 3, False, 5, False), (2, 4, False, 2, True)):
            added = total(edges.dx(across, x, back), edges.dz(down, x, up))
            out[comp, x] = velocity[comp, x] + speed * added

    over_rows(edges.nx, body)


def stress_edges(edges, stress, memory, stress_out, memory_out, props, then=None):
    inverse = 1.0 / edges.spacing

    def body(x):
        damp = props[DAMP, x]
        gain = DT - (0.5 * DT) * damp
        twice = inverse * props[MU2, x]
        half = 0.5 * twice

        def put(comp, rate):
            memory_out[comp, x] = memory[comp, x] if rate is None else memory[comp, x] - damp * rate
            stress_out[comp, x] = stress[comp, x] if rate is None else stress[comp, x] + gain * rate

        xx, zz = edges.dx(0, x, False), edges.dz(2, x, False)
        volume = inverse * props[LAME, x] * total(xx, zz)
        put(0, volume if xx is None else volume + twice * xx)
        put(1, volume)
        put(2, volume + twice * zz)
        xy = edges.dx(1, x, True)
        put(3, None if xy is None else half * xy)
        put(4, half * total(edges.dx(2, x, True), edges.dz(0, x, True)))
        put(5, half * edges.dz(1, x, True))
        if then is not None:
            then(x)

    over_rows(edges.nx, body)


def receive(sizes, halos, z_lists, interp, halo, lift):
    depO, diag, depE, latO, latE = halos
    xlo, xhi, zlo, zhi = halo
    lat, depth = lax.axis_index("lat"), lax.axis_index("depth")
    lat_even, depth_even = lax.rem(lat, 2) == 0, lax.rem(depth, 2) == 0
    last_lat, last_depth = sizes.lats - 1, sizes.depths - 1

    @pl.when(lat_even)
    def _():
        xlo[...] = latO[...]
        xhi[...] = latE[...]

    @pl.when(jnp.logical_not(lat_even))
    def _():
        xlo[...] = latE[...]
        xhi[...] = latO[...]

    @pl.when(lat == 0)
    def _():
        xlo[...] = jnp.zeros_like(xlo)

    @pl.when(lat == last_lat)
    def _():
        xhi[...] = jnp.zeros_like(xhi)

    @pl.when(depth_even)
    def _():
        zlo[...] = depO[...]
        zhi[...] = depE[...]

    @pl.when(jnp.logical_not(depth_even))
    def _():
        zlo[...] = depE[...]
        zhi[...] = depO[...]

    @pl.when(depth == 0)
    def _():
        zlo[0 : sizes.dep_fine, :] = jnp.zeros((sizes.dep_fine, sizes.fy), jnp.float32)

    @pl.when(depth == last_depth)
    def _():
        count = len(z_lists[1])
        lift[...] = jnp.zeros_like(lift)
        beyond = jnp.where(lat == last_lat, 0.0, 1.0)
        for k in range(count):
            planes = [depO[sizes.dep_slot(k, a)] for a in range(sizes.cx)]
            planes.append(diag[k : k + 1, :] * beyond)
            for a in range(sizes.cx):
                for p in range(3):
                    share = interp[0, p].astype(jnp.float32) * 0.125
                    x = k * sizes.fx + 3 * a + p
                    lift[x : x + 1, :] = share * planes[a] + (1.0 - share) * planes[a + 1]
        c = lax.broadcasted_iota(jnp.int32, (sizes.cy, sizes.fy), 0)
        f = lax.broadcasted_iota(jnp.int32, (sizes.cy, sizes.fy), 1)
        gap = f - 3 * c
        spread = jnp.zeros((sizes.cy, sizes.fy), jnp.float32)
        for p in range(3):
            share = interp[1, p].astype(jnp.float32) * 0.125
            spread = jnp.where(gap == p, share, spread)
            spread = jnp.where(gap == p - 3, 1.0 - share, spread)
        ghost = jnp.dot(
            lift[...], spread, precision=lax.Precision.HIGHEST, preferred_element_type=jnp.float32
        )
        zhi[...] = jnp.zeros_like(zhi)
        zhi[0 : sizes.dep_fine, :] = ghost[0 : sizes.dep_fine, :]


def send(sizes, fine, coarse, x_lists, z_lists, restrict, buffers, gather):
    depO, diag, depE, latO, latE = buffers
    lat, depth = lax.axis_index("lat"), lax.axis_index("depth")
    lat_even, depth_even = lax.rem(lat, 2) == 0, lax.rem(depth, 2) == 0
    last_depth = sizes.depths - 1

    def pack_x(up, down):
        for ref, entries, high in ((up, x_lists[0], True), (down, x_lists[1], False)):
            for k, (comp, r) in enumerate(entries):
                ref[k * sizes.fz : (k + 1) * sizes.fz, :] = fine[comp, sizes.fx - r if high else r]
                ref[sizes.lat_slot(k)] = coarse[comp, sizes.cx - r if high else r]

    def pack_z(up, down):
        for ref, entries, high in ((up, z_lists[0], True), (down, z_lists[1], False)):
            for k, (comp, r) in enumerate(entries):
                z = sizes.fz - r if high else r
                for x in range(sizes.fx):
                    ref[k * sizes.fx + x : k * sizes.fx + x + 1, :] = fine[comp, x, z : z + 1, :]
                z = sizes.cz - r if high else r
                for x in range(sizes.cx):
                    ref[sizes.dep_slot(k, x)] = coarse[comp, x, z : z + 1, :]

    @pl.when(lat_even)
    def _():
        pack_x(latE, latO)

    @pl.when(jnp.logical_not(lat_even))
    def _():
        pack_x(latO, latE)

    @pl.when(depth_even)
    def _():
        pack_z(depE, depO)

    @pl.when(jnp.logical_not(depth_even))
    def _():
        pack_z(depO, depE)

    diag[...] = jnp.zeros_like(diag)

    @pl.when(depth == 0)
    def _():
        for k, (comp, j) in enumerate(z_lists[1]):
            for x in range(sizes.cx):
                plane = ((2.0 - j) * coarse[comp, x, 0:1, :] + (1.0 + j) * coarse[comp, x, 1:2, :]) / 3.0
                depO[sizes.dep_slot(k, x)] = plane
                if x == 0:
                    diag[k : k + 1, :] = plane

    @pl.when(depth == last_depth)
    def _():
        wx = [restrict[0, p].astype(jnp.float32) for p in range(3)]
        wy = [restrict[1, p].astype(jnp.float32) for p in range(3)]
        gather[...] = jnp.zeros_like(gather)
        for k, (comp, r) in enumerate(z_lists[0]):
            z = sizes.fz - 3 * r
            for a in range(sizes.cx):
                total = None
                for p in range(3):
                    f = fine[comp, 3 * a + p, z : z + 3, :]
                    layers = wx[p] * (f[0:1] + f[1:2] + f[2:3])
                    total = layers if total is None else total + layers
                row = k * sizes.cx + a
                gather[row : row + 1, :] = total
        f = lax.broadcasted_iota(jnp.int32, (sizes.fy, sizes.cy), 0)
        c = lax.broadcasted_iota(jnp.int32, (sizes.fy, sizes.cy), 1)
        gap = f - 3 * c
        table = jnp.zeros((sizes.fy, sizes.cy), jnp.float32)
        for p in range(3):
            table = jnp.where(gap == p, wy[p], table)
        summed = jnp.dot(
            gather[...], table, precision=lax.Precision.HIGHEST, preferred_element_type=jnp.float32
        )
        norm = jnp.full((1, sizes.cy), 3.0 * (wx[0] + wx[1] + wx[2]) * (wy[0] + wy[1] + wy[2]))
        lifted = summed / norm
        for k in range(len(z_lists[0])):
            for a in range(sizes.cx):
                row = k * sizes.cx + a
                depO[sizes.dep_slot(k, a)] = lifted[row : row + 1, :]


SMEM = pl.BlockSpec(memory_space=pltpu.SMEM)
VMEM = pl.BlockSpec(memory_space=pltpu.VMEM)
HBM = pl.BlockSpec(memory_space=pltpu.HBM)
LIMIT = 24 * 1024 * 1024
PACK_LIMIT = 62 * 1024 * 1024
FIRST_LIMIT = 40 * 1024 * 1024


def packs(sizes):
    lat = jax.ShapeDtypeStruct((sizes.lat_rows, sizes.fy), jnp.float32)
    dep = jax.ShapeDtypeStruct((sizes.dep_rows, sizes.fy), jnp.float32)
    return [dep, jax.ShapeDtypeStruct((8, sizes.cy), jnp.float32), dep, lat, lat]


def halo_scratch(sizes):
    lat = pltpu.VMEM((sizes.lat_rows, sizes.fy), jnp.float32)
    dep = pltpu.VMEM((sizes.dep_rows, sizes.fy), jnp.float32)
    return [lat, lat, dep, dep, pltpu.VMEM((-(-sizes.dep_fine // 8) * 8, sizes.cy), jnp.float32)]


def gather_scratch(sizes):
    return pltpu.VMEM((-(-5 * sizes.cx // 8) * 8, sizes.fy), jnp.float32)


def like(x):
    return jax.ShapeDtypeStruct(x.shape, x.dtype)


def call(kernel, name, smem, vmem, outs, scratch, work, far=(), far_outs=(), limit=LIMIT):
    outs = [*far_outs, *outs]
    moved = sum(x.size * 4 for x in (*far, *vmem)) + sum(4 * o.size for o in outs)
    return pl.pallas_call(
        kernel,
        name=name,
        out_shape=outs,
        in_specs=[SMEM] * len(smem) + [HBM] * len(far) + [VMEM] * len(vmem),
        out_specs=[HBM] * len(far_outs) + [VMEM] * (len(outs) - len(far_outs)),
        scratch_shapes=scratch,
        compiler_params=pltpu.CompilerParams(vmem_limit_bytes=limit),
        cost_estimate=pl.CostEstimate(flops=work, bytes_accessed=moved, transcendentals=0),
    )(*smem, *far, *vmem)


def room(x):
    return pltpu.VMEM(x.shape, x.dtype)


def pack_stress(sizes, restrict, fine, coarse):
    def kernel(restrict, fine, coarse, *rest):
        buffers, (gather, near_fine, near_coarse, sems) = rest[:5], rest[5:]
        fx = sizes.fx
        copies = []
        for source, target, part in (
            (fine, near_fine, (slice(4, 6),)),
            (fine, near_fine, (2,)),
            (coarse, near_coarse, (slice(2, 6),)),
            (coarse, near_coarse, (0,)),
            (fine, near_fine, (0, slice(0, 2))),
            (fine, near_fine, (0, slice(fx - 1, fx))),
            (fine, near_fine, (3, slice(0, 1))),
            (fine, near_fine, (3, slice(fx - 2, fx))),
        ):
            copies.append(pltpu.make_async_copy(source.at[part], target.at[part], sems.at[len(copies)]))
        for copy in copies:
            copy.start()
        for copy in copies:
            copy.wait()
        send(sizes, near_fine, near_coarse, STRESS_X, STRESS_Z, restrict, buffers, gather)

    scratch = [gather_scratch(sizes), room(fine), room(coarse), pltpu.SemaphoreType.DMA((8,))]
    return call(
        kernel, "pack_stress", (restrict,), (), packs(sizes), scratch, 10**6, far=(fine, coarse), limit=PACK_LIMIT
    )


def material_rows(table, zone, out):
    def step(x, carry):
        kind = zone[x]

        def column(index):
            value = jnp.full(kind.shape, table[7, index])
            for level in range(7):
                value = jnp.where(kind == level, table[level, index], value)
            return value

        lame, shear, decay = column(1), column(2), column(3)
        out[CB, x] = column(0)
        out[LAME, x] = lame
        out[MU2, x] = 2.0 * shear
        out[DECAY, x] = decay
        out[DAMP, x] = column(4) * (1.0 - decay)
        out[ISO, x] = lame / (3.0 * lame + 2.0 * shear)
        out[SCALE, x] = 0.5 / shear
        return carry

    lax.fori_loop(0, zone.shape[0], step, 0)


def first_bulk(table, zones, stress, velocity):
    def kernel(table, *rest):
        far, (of, oc, pf, pc), near, sems = rest[:6], rest[6:10], rest[10:16], rest[16]
        copies = [pltpu.make_async_copy(a, b, sems.at[i]) for i, (a, b) in enumerate(zip(far, near))]
        for copy in copies:
            copy.start()
        zf, zc, sf, sc, vf, vc = near
        copies[0].wait()
        material_rows(table, zf, pf)
        copies[1].wait()
        material_rows(table, zc, pc)
        for copy in copies[2:]:
            copy.wait()
        velocity_rows(Grid(sf, 1.0), vf, of, pf)
        velocity_rows(Grid(sc, 3.0), vc, oc, pc)

    outs = [like(v) for v in velocity]
    outs += [jax.ShapeDtypeStruct((7,) + z.shape, jnp.float32) for z in zones]
    far = (*zones, *stress, *velocity)
    scratch = [room(x) for x in far] + [pltpu.SemaphoreType.DMA((6,))]
    out = call(kernel, "first_bulk", (table,), (), outs, scratch, BULK, far=far, limit=FIRST_LIMIT)
    return out[:2], out[2:]


def velocity_bulk(stress, props, velocity, peak):
    def kernel(sf, sc, pf, pc, vf, vc, *rest):
        kf, kc, of, oc, okf, okc = rest
        velocity_rows(Grid(sf, 1.0), vf, of, pf)
        velocity_rows(Grid(sc, 3.0), vc, oc, pc)
        peak_rows(sf, pf, kf, okf)
        peak_rows(sc, pc, kc, okc)

    outs = [like(x) for x in (*velocity, *peak)]
    out = call(kernel, "velocity_bulk", (), (*stress, *props, *velocity, *peak), outs, [], BULK)
    return out[:2], out[2:]


def stress_bulk(velocity, props, stress, memory):
    def kernel(vf, vc, pf, pc, sf, sc, mf, mc, osf, osc, omf, omc):
        stress_rows(Grid(vf, 1.0), sf, mf, osf, omf, pf)
        stress_rows(Grid(vc, 3.0), sc, mc, osc, omc, pc)

    outs = [like(x) for x in (*stress, *memory)]
    return call(kernel, "stress_bulk", (), (*velocity, *props, *stress, *memory), outs, [], BULK)


def velocity_finish(sizes, interp, restrict, halos, props, velocity):
    def kernel(interp, restrict, *rest):
        halos, (pf, pc), (vf, vc), (of, oc), buffers = rest[:5], rest[5:7], rest[7:9], rest[9:11], rest[11:16]
        halo, (lift, gather) = rest[16:20], rest[20:]
        receive(sizes, halos, STRESS_Z, interp, halo, lift)
        velocity_edges(Edges(sizes, True, STRESS_X, STRESS_Z, halo), vf, of, pf)
        velocity_edges(Edges(sizes, False, STRESS_X, STRESS_Z, halo), vc, oc, pc)
        send(sizes, of, oc, VELOCITY_X, VELOCITY_Z, restrict, buffers, gather)

    outs = [like(v) for v in velocity] + packs(sizes)
    out = call(
        kernel, "velocity_finish", (interp, restrict), (*halos, *props, *velocity), outs,
        halo_scratch(sizes) + [gather_scratch(sizes)], 10**7,
    )
    return out[:2], out[2:]


def stress_finish(sizes, interp, restrict, halos, props, stress, memory):
    def kernel(interp, restrict, *rest):
        halos, (pf, pc), (sf, sc, mf, mc), (osf, osc, omf, omc) = rest[:5], rest[5:7], rest[7:11], rest[11:15]
        outgoing, halo, (lift, gather) = rest[15:20], rest[20:24], rest[24:]
        receive(sizes, halos, VELOCITY_Z, interp, halo, lift)
        stress_edges(Edges(sizes, True, VELOCITY_X, VELOCITY_Z, halo), sf, mf, osf, omf, pf)
        stress_edges(Edges(sizes, False, VELOCITY_X, VELOCITY_Z, halo), sc, mc, osc, omc, pc)
        send(sizes, osf, osc, STRESS_X, STRESS_Z, restrict, outgoing, gather)

    outs = [like(x) for x in (*stress, *memory)] + packs(sizes)
    out = call(
        kernel, "stress_finish", (interp, restrict), (*halos, *props, *stress, *memory), outs,
        halo_scratch(sizes) + [gather_scratch(sizes)], 2 * 10**7,
    )
    return out[:2], out[2:4], out[4:]


def last_finish(sizes, interp, halos, props, stress, memory, peak, velocity):
    def kernel(interp, *rest):
        halos, (pf, pc), (sf, sc, mf, mc), (kf, kc), speeds = rest[:5], rest[5:7], rest[7:11], rest[11:13], rest[13:15]
        outs, halo, lift = rest[15:23], rest[23:27], rest[27]
        near, sems = rest[28:34], rest[34]

        def whole(i):
            source = speeds[i] if i < 2 else near[i - 2]
            return pltpu.make_async_copy(source, outs[i], sems.at[i])

        for i in range(2):
            whole(i).start()
        receive(sizes, halos, VELOCITY_Z, interp, halo, lift)
        osf, osc, omf, omc, okf, okc = near

        def store(x):
            for i in (2, 4):
                pltpu.make_async_copy(near[i - 2].at[:, x], outs[i].at[:, x], sems.at[i]).start()

        stress_edges(Edges(sizes, True, VELOCITY_X, VELOCITY_Z, halo), sf, mf, osf, omf, pf, store)
        stress_edges(Edges(sizes, False, VELOCITY_X, VELOCITY_Z, halo), sc, mc, osc, omc, pc)
        for i in (3, 5):
            whole(i).start()
        peak_rows(osf, pf, kf, okf)
        whole(6).start()
        peak_rows(osc, pc, kc, okc)
        whole(7).start()
        for i in range(8):
            whole(i).wait()

    outs = [like(x) for x in (*velocity, *stress, *memory, *peak)]
    scratch = halo_scratch(sizes) + [room(x) for x in (*stress, *memory, *peak)] + [pltpu.SemaphoreType.DMA((8,))]
    out = call(
        kernel, "last_finish", (interp,), (*halos, *props, *stress, *memory, *peak, *velocity), [],
        scratch, 2 * 10**7, far_outs=outs,
    )
    return out[:2], out[2:4], out[4:6], out[6:]


def rotation(low, high, pivot):
    gap = high - low
    twice = pivot + pivot
    square = twice * twice
    length2 = jnp.maximum(gap * gap + square, TINY)
    length = length2 * lax.rsqrt(length2)
    signed = jnp.where(gap >= 0, length, -length)
    middle = 0.5 * (low + high)
    reach = 0.5 * signed
    base = gap + signed

    def turn():
        inverse = lax.rsqrt(base * base + square)
        return base * inverse, twice * inverse

    return middle - reach, middle + reach, turn


def largest_eigenvalue(a, b, c, ab, ac, bc):
    a, b, turn = rotation(a, b, ab)
    cosine, sine = turn()
    ac, bc = cosine * ac - sine * bc, sine * ac + cosine * bc
    for sweep in range(3):
        if sweep > 0:
            a, b, turn = rotation(a, b, ab)
            cosine, sine = turn()
            ac, bc = cosine * ac, sine * ac
        a, c, turn = rotation(a, c, ac)
        cosine, sine = turn()
        ab, bc = -(sine * bc), cosine * bc
        b, c, turn = rotation(b, c, bc)
        if sweep < 2:
            cosine, sine = turn()
            ab, ac = cosine * ab, sine * ab
    return jnp.maximum(jnp.maximum(a, b), c)


def peak_rows(stress, props, peak, out, width=2):
    def step(i, carry):
        x = pl.ds(i * width, width)
        xx, yy, zz, xy, xz, yz = [stress[comp, x] for comp in range(6)]
        top = largest_eigenvalue(xx, yy, zz, xy, xz, yz)
        principal = (top - props[ISO, x] * (xx + yy + zz)) * props[SCALE, x]
        out[x] = jnp.maximum(peak[x], principal)
        return carry

    lax.fori_loop(0, stress.shape[1] // width, step, 0)


def exchanged(arrays):
    depO, diag, depE, latO, latE = arrays
    lat, depth = lax.axis_size("lat"), lax.axis_size("depth")

    def swaps(count, first):
        pairs = [(i, (i + 1) % count) for i in range(first, count, 2)]
        return pairs + [(b, a) for a, b in pairs]

    across = [((i + 1) * depth, i * depth + depth - 1) for i in range(lat - 1)]
    depO = lax.ppermute(depO, "depth", swaps(depth, 1))
    diag = lax.ppermute(diag, ("lat", "depth"), across)
    depE = lax.ppermute(depE, "depth", swaps(depth, 0))
    latO = lax.ppermute(latO, "lat", swaps(lat, 1))
    latE = lax.ppermute(latE, "lat", swaps(lat, 0))
    return (depO, diag, depE, latO, latE)


def on_device(
    velocity_fine,
    stress_fine,
    memory_fine,
    peak_fine,
    zone_fine,
    velocity_coarse,
    stress_coarse,
    memory_coarse,
    peak_coarse,
    zone_coarse,
    zone_table,
    interp_weight,
    restrict_weight,
):
    sizes = Sizes(stress_fine.shape[1:], stress_coarse.shape[1:])
    velocity = (velocity_fine, velocity_coarse)
    stress = (stress_fine, stress_coarse)
    memory = (memory_fine, memory_coarse)
    peak = (peak_fine, peak_coarse)
    outgoing = pack_stress(sizes, restrict_weight, *stress)
    for step in range(STEPS):
        halos = exchanged(outgoing)
        if step == 0:
            velocity, props = first_bulk(zone_table, (zone_fine, zone_coarse), stress, velocity)
        else:
            velocity, peak = velocity_bulk(stress, props, velocity, peak)
        velocity, outgoing = velocity_finish(
            sizes, interp_weight, restrict_weight, halos, props, velocity
        )
        halos = exchanged(outgoing)
        bulk = stress_bulk(velocity, props, stress, memory)
        if step + 1 < STEPS:
            stress, memory, outgoing = stress_finish(
                sizes, interp_weight, restrict_weight, halos, props, bulk[:2], bulk[2:]
            )
        else:
            velocity, stress, memory, peak = last_finish(
                sizes, interp_weight, halos, props, bulk[:2], bulk[2:], peak, velocity
            )
    return (velocity[0], stress[0], memory[0], peak[0], velocity[1], stress[1], memory[1], peak[1])


def solution(mesh):
    field = P(None, "lat", "depth", None)
    scalar = P("lat", "depth", None)
    grid = (field, field, field, scalar)
    return jax.shard_map(
        on_device,
        mesh=mesh,
        in_specs=(*grid, scalar, *grid, scalar, P(), P(), P()),
        out_specs=(*grid, *grid),
        check_vma=False,
    )
```

```python
import functools

import jax
import jax.numpy as jnp
from jax import lax
from jax.experimental import pallas as pl
from jax.experimental.pallas import tpu as pltpu
from jax.sharding import PartitionSpec as P

STEPS = 2
DT = 0.4
NEAR = 9.0 / 8.0
FAR = 1.0 / 24.0
TINY = 1e-36

STRESS_X = ([(0, 1), (3, 2), (3, 1), (4, 2), (4, 1)], [(0, 0), (0, 1), (3, 0), (4, 0)])
STRESS_Z = ([(4, 2), (4, 1), (5, 2), (5, 1), (2, 1)], [(4, 0), (5, 0), (2, 0), (2, 1)])
VELOCITY_X = ([(0, 2), (0, 1), (1, 1), (2, 1)], [(0, 0), (1, 0), (1, 1), (2, 0), (2, 1)])
VELOCITY_Z = ([(2, 2), (2, 1), (0, 1), (1, 1)], [(2, 0), (0, 0), (0, 1), (1, 0), (1, 1)])

BULK = 2 * 10**6
EARLY = 8
CB, LAME, MU2, DECAY, DAMP, ISO, SCALE = range(7)


class Sizes:
    def __init__(self, fine, coarse):
        self.lats, self.depths = lax.axis_size("lat"), lax.axis_size("depth")
        self.fx, self.fz, self.fy = fine
        self.cx, self.cz, self.cy = coarse
        self.lanes = self.fy // self.cy
        self.lat_fine = 5 * self.fz
        self.lat_rows = self.lat_fine + -(-5 // self.lanes) * self.cz
        self.dep_fine = 5 * self.fx
        used = self.dep_fine + 5 * -(-self.cx // self.lanes)
        self.dep_rows = -(-used // 8) * 8

    def lat_slot(self, k):
        row = self.lat_fine + (k // self.lanes) * self.cz
        lane = (k % self.lanes) * self.cy
        return (slice(row, row + self.cz), slice(lane, lane + self.cy))

    def dep_slot(self, k, x):
        row = self.dep_fine + (x // self.lanes) * 5 + k
        lane = (x % self.lanes) * self.cy
        return (slice(row, row + 1), slice(lane, lane + self.cy))


def y_shift(f, offset, lane):
    width = f.shape[1]
    moved = pltpu.roll(f, (-offset) % width, 1)
    inside = lane < width - offset if offset > 0 else lane >= -offset
    return jnp.where(inside, moved, 0.0)


def z_shift(f, offset, row):
    depth = f.shape[0]
    moved = pltpu.roll(f, (-offset) % depth, 0)
    inside = row < depth - offset if offset > 0 else row >= -offset
    return jnp.where(inside, moved, 0.0)


def parts(at, up):
    def minus(a, b):
        if a is None or b is None:
            return a if b is None else -b
        return a - b

    if up:
        return minus(at(1), at(0)), minus(at(2), at(-1))
    return minus(at(0), at(-1)), minus(at(1), at(-2))


class Grid:
    def __init__(self, field, spacing):
        self.field, self.spacing = field, spacing
        _, self.nx, self.nz, self.ny = field.shape
        self.row = lax.broadcasted_iota(jnp.int32, (self.nz, self.ny), 0)
        self.lane = lax.broadcasted_iota(jnp.int32, (self.nz, self.ny), 1)

    def dx(self, comp, x, up):
        def at(offset):
            if isinstance(x, int) and not 0 <= x + offset < self.nx:
                return None
            return self.field[comp, x + offset]

        return parts(at, up)

    def dy(self, comp, x, up):
        f = self.field[comp, x]
        return parts(lambda offset: y_shift(f, offset, self.lane) if offset else f, up)

    def dz(self, comp, x, up):
        f = self.field[comp, x]
        return parts(lambda offset: z_shift(f, offset, self.row) if offset else f, up)


def over_rows(count, body):
    if count <= 8:
        for x in range(count):
            body(x)
        return

    def step(x, carry):
        body(x)
        return carry

    for x in (0, 1):
        body(x)
    lax.fori_loop(2, count - 2, step, 0)
    for x in (count - 2, count - 1):
        body(x)


def combine(*pairs):
    near = [p[0] for p in pairs if p[0] is not None]
    far = [p[1] for p in pairs if p[1] is not None]
    return NEAR * functools.reduce(jnp.add, near) - FAR * functools.reduce(jnp.add, far)


def velocity_rows(grid, velocity, out, props):
    scale = DT / grid.spacing

    def body(x):
        speed = scale * props[CB, x]
        ax = combine(grid.dx(0, x, True), grid.dy(3, x, False), grid.dz(4, x, False))
        out[0, x] = velocity[0, x] + speed * ax
        ay = combine(grid.dx(3, x, False), grid.dy(1, x, True), grid.dz(5, x, False))
        out[1, x] = velocity[1, x] + speed * ay
        az = combine(grid.dx(4, x, False), grid.dy(5, x, False), grid.dz(2, x, True))
        out[2, x] = velocity[2, x] + speed * az

    over_rows(grid.nx, body)


def stress_rows(grid, stress, memory, stress_out, memory_out, props):
    inverse = 1.0 / grid.spacing

    def body(x):
        lame, twice = props[LAME, x], props[MU2, x]
        decay, damp = props[DECAY, x], props[DAMP, x]
        if inverse != 1.0:
            lame, twice = lame * inverse, twice * inverse
        half = 0.5 * twice

        def finish(comp, rate):
            old = memory[comp, x]
            new = decay * old - damp * rate
            memory_out[comp, x] = new
            stress_out[comp, x] = stress[comp, x] + DT * (rate + 0.5 * (old + new))

        xx = combine(grid.dx(0, x, False))
        yy = combine(grid.dy(1, x, False))
        zz = combine(grid.dz(2, x, False))
        volume = lame * (xx + yy + zz)
        finish(0, volume + twice * xx)
        finish(1, volume + twice * yy)
        finish(2, volume + twice * zz)
        finish(3, half * combine(grid.dy(0, x, True), grid.dx(1, x, True)))
        finish(4, half * combine(grid.dz(0, x, True), grid.dx(2, x, True)))
        finish(5, half * combine(grid.dz(1, x, True), grid.dy(2, x, True)))

    over_rows(grid.nx, body)


class Edges:
    def __init__(self, sizes, fine, x_lists, z_lists, halo):
        self.sizes, self.fine = sizes, fine
        self.x_lists, self.z_lists = x_lists, z_lists
        self.xlo, self.xhi, self.zlo, self.zhi = halo
        self.nx, self.nz, self.ny = (
            (sizes.fx, sizes.fz, sizes.fy) if fine else (sizes.cx, sizes.cz, sizes.cy)
        )
        self.spacing = 1.0 if fine else 3.0
        self.row = lax.broadcasted_iota(jnp.int32, (8, self.ny), 0)

    def x_layer(self, ref, k):
        if self.fine:
            return ref[k * self.nz : (k + 1) * self.nz, :]
        return ref[self.sizes.lat_slot(k)]

    def low_x(self, comp, r):
        return self.x_layer(self.xlo, self.x_lists[0].index((comp, r)))

    def high_x(self, comp, r):
        return self.x_layer(self.xhi, self.x_lists[1].index((comp, r)))

    def dx(self, comp, x, up):
        if not isinstance(x, int):
            return None
        back = x - (self.nx - 1)
        if up:
            terms = {0: lambda: FAR * self.low_x(comp, 1)}
            ends = {
                0: lambda: NEAR * self.high_x(comp, 0) - FAR * self.high_x(comp, 1),
                -1: lambda: -FAR * self.high_x(comp, 0),
            }
        else:
            terms = {
                0: lambda: FAR * self.low_x(comp, 2) - NEAR * self.low_x(comp, 1),
                1: lambda: FAR * self.low_x(comp, 1),
            }
            ends = {0: lambda: -FAR * self.high_x(comp, 0)}
        found = [f() for f in (terms.get(x), ends.get(back)) if f is not None]
        return functools.reduce(jnp.add, found) if found else None

    def z_row(self, ref, k, x):
        if not self.fine:
            return ref[self.sizes.dep_slot(k, x)]
        if isinstance(x, int):
            return ref[k * self.nx + x : k * self.nx + x + 1, :]
        return ref[pl.ds(k * self.nx + x, 1), :]

    def dz(self, comp, x, up):
        low = {r: self.z_row(self.zlo, k, x) for k, (c, r) in enumerate(self.z_lists[0]) if c == comp}
        high = {r: self.z_row(self.zhi, k, x) for k, (c, r) in enumerate(self.z_lists[1]) if c == comp}
        row = self.row
        if up:
            top = jnp.where(row == 0, FAR * low[1], 0.0)
            bottom = jnp.where(
                row == 7, NEAR * high[0] - FAR * high[1], jnp.where(row == 6, -FAR * high[0], 0.0)
            )
        else:
            top = jnp.where(row == 0, FAR * low[2] - NEAR * low[1], jnp.where(row == 1, FAR * low[1], 0.0))
            bottom = jnp.where(row == 7, -FAR * high[0], 0.0)
        middle = [jnp.zeros((self.nz - 16, self.ny), jnp.float32)] if self.nz > 16 else []
        return jnp.concatenate([top, *middle, bottom], axis=0)


def total(*terms):
    found = [t for t in terms if t is not None]
    return functools.reduce(jnp.add, found) if found else None


def velocity_edges(edges, velocity, out, props):
    scale = DT / edges.spacing

    def body(x):
        speed = scale * props[CB, x]
        for comp, across, back, down, up in ((0, 0, True, 4, False), (1, 3, False, 5, False), (2, 4, False, 2, True)):
            added = total(edges.dx(across, x, back), edges.dz(down, x, up))
            out[comp, x] = velocity[comp, x] + speed * added

    over_rows(edges.nx, body)


def stress_edges(edges, stress, memory, stress_out, memory_out, props, then=None):
    inverse = 1.0 / edges.spacing

    def body(x):
        damp = props[DAMP, x]
        gain = DT - (0.5 * DT) * damp
        twice = inverse * props[MU2, x]
        half = 0.5 * twice

        def put(comp, rate):
            memory_out[comp, x] = memory[comp, x] if rate is None else memory[comp, x] - damp * rate
            stress_out[comp, x] = stress[comp, x] if rate is None else stress[comp, x] + gain * rate

        xx, zz = edges.dx(0, x, False), edges.dz(2, x, False)
        volume = inverse * props[LAME, x] * total(xx, zz)
        put(0, volume if xx is None else volume + twice * xx)
        put(1, volume)
        put(2, volume + twice * zz)
        xy = edges.dx(1, x, True)
        put(3, None if xy is None else half * xy)
        put(4, half * total(edges.dx(2, x, True), edges.dz(0, x, True)))
        put(5, half * edges.dz(1, x, True))
        if then is not None:
            then(x)

    over_rows(edges.nx, body)


def receive(sizes, halos, z_lists, interp, halo, lift):
    depO, diag, depE, latO, latE = halos
    xlo, xhi, zlo, zhi = halo
    lat, depth = lax.axis_index("lat"), lax.axis_index("depth")
    lat_even, depth_even = lax.rem(lat, 2) == 0, lax.rem(depth, 2) == 0
    last_lat, last_depth = sizes.lats - 1, sizes.depths - 1

    @pl.when(lat_even)
    def _():
        xlo[...] = latO[...]
        xhi[...] = latE[...]

    @pl.when(jnp.logical_not(lat_even))
    def _():
        xlo[...] = latE[...]
        xhi[...] = latO[...]

    @pl.when(lat == 0)
    def _():
        xlo[...] = jnp.zeros_like(xlo)

    @pl.when(lat == last_lat)
    def _():
        xhi[...] = jnp.zeros_like(xhi)

    @pl.when(depth_even)
    def _():
        zlo[...] = depO[...]
        zhi[...] = depE[...]

    @pl.when(jnp.logical_not(depth_even))
    def _():
        zlo[...] = depE[...]
        zhi[...] = depO[...]

    @pl.when(depth == 0)
    def _():
        zlo[0 : sizes.dep_fine, :] = jnp.zeros((sizes.dep_fine, sizes.fy), jnp.float32)

    @pl.when(depth == last_depth)
    def _():
        count = len(z_lists[1])
        lift[...] = jnp.zeros_like(lift)
        beyond = jnp.where(lat == last_lat, 0.0, 1.0)
        for k in range(count):
            planes = [depO[sizes.dep_slot(k, a)] for a in range(sizes.cx)]
            planes.append(diag[k : k + 1, :] * beyond)
            for a in range(sizes.cx):
                for p in range(3):
                    share = interp[0, p].astype(jnp.float32) * 0.125
                    x = k * sizes.fx + 3 * a + p
                    lift[x : x + 1, :] = share * planes[a] + (1.0 - share) * planes[a + 1]
        c = lax.broadcasted_iota(jnp.int32, (sizes.cy, sizes.fy), 0)
        f = lax.broadcasted_iota(jnp.int32, (sizes.cy, sizes.fy), 1)
        gap = f - 3 * c
        spread = jnp.zeros((sizes.cy, sizes.fy), jnp.float32)
        for p in range(3):
            share = interp[1, p].astype(jnp.float32) * 0.125
            spread = jnp.where(gap == p, share, spread)
            spread = jnp.where(gap == p - 3, 1.0 - share, spread)
        ghost = jnp.dot(
            lift[...], spread, precision=lax.Precision.HIGHEST, preferred_element_type=jnp.float32
        )
        zhi[...] = jnp.zeros_like(zhi)
        zhi[0 : sizes.dep_fine, :] = ghost[0 : sizes.dep_fine, :]


def send(sizes, fine, coarse, x_lists, z_lists, restrict, buffers, gather):
    depO, diag, depE, latO, latE = buffers
    lat, depth = lax.axis_index("lat"), lax.axis_index("depth")
    lat_even, depth_even = lax.rem(lat, 2) == 0, lax.rem(depth, 2) == 0
    last_depth = sizes.depths - 1

    def pack_x(up, down):
        for ref, entries, high in ((up, x_lists[0], True), (down, x_lists[1], False)):
            for k, (comp, r) in enumerate(entries):
                ref[k * sizes.fz : (k + 1) * sizes.fz, :] = fine[comp, sizes.fx - r if high else r]
                ref[sizes.lat_slot(k)] = coarse[comp, sizes.cx - r if high else r]

    def pack_z(up, down):
        for ref, entries, high in ((up, z_lists[0], True), (down, z_lists[1], False)):
            for k, (comp, r) in enumerate(entries):
                z = sizes.fz - r if high else r
                for x in range(sizes.fx):
                    ref[k * sizes.fx + x : k * sizes.fx + x + 1, :] = fine[comp, x, z : z + 1, :]
                z = sizes.cz - r if high else r
                for x in range(sizes.cx):
                    ref[sizes.dep_slot(k, x)] = coarse[comp, x, z : z + 1, :]

    @pl.when(lat_even)
    def _():
        pack_x(latE, latO)

    @pl.when(jnp.logical_not(lat_even))
    def _():
        pack_x(latO, latE)

    @pl.when(depth_even)
    def _():
        pack_z(depE, depO)

    @pl.when(jnp.logical_not(depth_even))
    def _():
        pack_z(depO, depE)

    diag[...] = jnp.zeros_like(diag)

    @pl.when(depth == 0)
    def _():
        for k, (comp, j) in enumerate(z_lists[1]):
            for x in range(sizes.cx):
                plane = ((2.0 - j) * coarse[comp, x, 0:1, :] + (1.0 + j) * coarse[comp, x, 1:2, :]) / 3.0
                depO[sizes.dep_slot(k, x)] = plane
                if x == 0:
                    diag[k : k + 1, :] = plane

    @pl.when(depth == last_depth)
    def _():
        wx = [restrict[0, p].astype(jnp.float32) for p in range(3)]
        wy = [restrict[1, p].astype(jnp.float32) for p in range(3)]
        gather[...] = jnp.zeros_like(gather)
        for k, (comp, r) in enumerate(z_lists[0]):
            z = sizes.fz - 3 * r
            for a in range(sizes.cx):
                total = None
                for p in range(3):
                    f = fine[comp, 3 * a + p, z : z + 3, :]
                    layers = wx[p] * (f[0:1] + f[1:2] + f[2:3])
                    total = layers if total is None else total + layers
                row = k * sizes.cx + a
                gather[row : row + 1, :] = total
        f = lax.broadcasted_iota(jnp.int32, (sizes.fy, sizes.cy), 0)
        c = lax.broadcasted_iota(jnp.int32, (sizes.fy, sizes.cy), 1)
        gap = f - 3 * c
        table = jnp.zeros((sizes.fy, sizes.cy), jnp.float32)
        for p in range(3):
            table = jnp.where(gap == p, wy[p], table)
        summed = jnp.dot(
            gather[...], table, precision=lax.Precision.HIGHEST, preferred_element_type=jnp.float32
        )
        norm = jnp.full((1, sizes.cy), 3.0 * (wx[0] + wx[1] + wx[2]) * (wy[0] + wy[1] + wy[2]))
        lifted = summed / norm
        for k in range(len(z_lists[0])):
            for a in range(sizes.cx):
                row = k * sizes.cx + a
                depO[sizes.dep_slot(k, a)] = lifted[row : row + 1, :]


SMEM = pl.BlockSpec(memory_space=pltpu.SMEM)
VMEM = pl.BlockSpec(memory_space=pltpu.VMEM)
HBM = pl.BlockSpec(memory_space=pltpu.HBM)
LIMIT = 24 * 1024 * 1024
PACK_LIMIT = 62 * 1024 * 1024
FIRST_LIMIT = 40 * 1024 * 1024


def packs(sizes):
    lat = jax.ShapeDtypeStruct((sizes.lat_rows, sizes.fy), jnp.float32)
    dep = jax.ShapeDtypeStruct((sizes.dep_rows, sizes.fy), jnp.float32)
    return [dep, jax.ShapeDtypeStruct((8, sizes.cy), jnp.float32), dep, lat, lat]


def halo_scratch(sizes):
    lat = pltpu.VMEM((sizes.lat_rows, sizes.fy), jnp.float32)
    dep = pltpu.VMEM((sizes.dep_rows, sizes.fy), jnp.float32)
    return [lat, lat, dep, dep, pltpu.VMEM((-(-sizes.dep_fine // 8) * 8, sizes.cy), jnp.float32)]


def gather_scratch(sizes):
    return pltpu.VMEM((-(-5 * sizes.cx // 8) * 8, sizes.fy), jnp.float32)


def like(x):
    return jax.ShapeDtypeStruct(x.shape, x.dtype)


def call(kernel, name, smem, vmem, outs, scratch, work, far=(), far_outs=(), limit=LIMIT):
    outs = [*far_outs, *outs]
    moved = sum(x.size * 4 for x in (*far, *vmem)) + sum(4 * o.size for o in outs)
    return pl.pallas_call(
        kernel,
        name=name,
        out_shape=outs,
        in_specs=[SMEM] * len(smem) + [HBM] * len(far) + [VMEM] * len(vmem),
        out_specs=[HBM] * len(far_outs) + [VMEM] * (len(outs) - len(far_outs)),
        scratch_shapes=scratch,
        compiler_params=pltpu.CompilerParams(vmem_limit_bytes=limit),
        cost_estimate=pl.CostEstimate(flops=work, bytes_accessed=moved, transcendentals=0),
    )(*smem, *far, *vmem)


def room(x):
    return pltpu.VMEM(x.shape, x.dtype)


def pack_stress(sizes, restrict, fine, coarse):
    def kernel(restrict, fine, coarse, *rest):
        buffers, (gather, near_fine, near_coarse, sems) = rest[:5], rest[5:]
        fx = sizes.fx
        copies = []
        for source, target, part in (
            (fine, near_fine, (slice(4, 6),)),
            (fine, near_fine, (2,)),
            (coarse, near_coarse, (slice(2, 6),)),
            (coarse, near_coarse, (0,)),
            (fine, near_fine, (0, slice(0, 2))),
            (fine, near_fine, (0, slice(fx - 1, fx))),
            (fine, near_fine, (3, slice(0, 1))),
            (fine, near_fine, (3, slice(fx - 2, fx))),
        ):
            copies.append(pltpu.make_async_copy(source.at[part], target.at[part], sems.at[len(copies)]))
        for copy in copies:
            copy.start()
        for copy in copies:
            copy.wait()
        send(sizes, near_fine, near_coarse, STRESS_X, STRESS_Z, restrict, buffers, gather)

    scratch = [gather_scratch(sizes), room(fine), room(coarse), pltpu.SemaphoreType.DMA((8,))]
    return call(
        kernel, "pack_stress", (restrict,), (), packs(sizes), scratch, 10**6, far=(fine, coarse), limit=PACK_LIMIT
    )


def material_rows(table, zone, out):
    def step(x, carry):
        kind = zone[x]

        def column(index):
            value = jnp.full(kind.shape, table[7, index])
            for level in range(7):
                value = jnp.where(kind == level, table[level, index], value)
            return value

        lame, shear, decay = column(1), column(2), column(3)
        out[CB, x] = column(0)
        out[LAME, x] = lame
        out[MU2, x] = 2.0 * shear
        out[DECAY, x] = decay
        out[DAMP, x] = column(4) * (1.0 - decay)
        out[ISO, x] = lame / (3.0 * lame + 2.0 * shear)
        out[SCALE, x] = 0.5 / shear
        return carry

    lax.fori_loop(0, zone.shape[0], step, 0)


def first_bulk(table, zones, stress, velocity):
    def kernel(table, *rest):
        far, (of, oc, pf, pc), near, sems = rest[:6], rest[6:10], rest[10:16], rest[16]
        copies = [pltpu.make_async_copy(a, b, sems.at[i]) for i, (a, b) in enumerate(zip(far, near))]
        for copy in copies:
            copy.start()
        zf, zc, sf, sc, vf, vc = near
        copies[0].wait()
        material_rows(table, zf, pf)
        copies[1].wait()
        material_rows(table, zc, pc)
        for copy in copies[2:]:
            copy.wait()
        velocity_rows(Grid(sf, 1.0), vf, of, pf)
        velocity_rows(Grid(sc, 3.0), vc, oc, pc)

    outs = [like(v) for v in velocity]
    outs += [jax.ShapeDtypeStruct((7,) + z.shape, jnp.float32) for z in zones]
    far = (*zones, *stress, *velocity)
    scratch = [room(x) for x in far] + [pltpu.SemaphoreType.DMA((6,))]
    out = call(kernel, "first_bulk", (table,), (), outs, scratch, BULK, far=far, limit=FIRST_LIMIT)
    return out[:2], out[2:]


def velocity_bulk(stress, props, velocity, peak):
    def kernel(sf, sc, pf, pc, vf, vc, *rest):
        kf, of, oc, okf = rest
        velocity_rows(Grid(sf, 1.0), vf, of, pf)
        velocity_rows(Grid(sc, 3.0), vc, oc, pc)
        peak_rows(sf, pf, kf, okf, 0, EARLY)

    outs = [like(x) for x in (*velocity, peak[0])]
    out = call(kernel, "velocity_bulk", (), (*stress, *props, *velocity, peak[0]), outs, [], BULK)
    return out[:2], out[2]


def stress_bulk(velocity, props, stress, memory, peak=(), early=None):
    def kernel(vf, vc, pf, pc, sf, sc, mf, mc, *rest):
        osf, osc, omf, omc = rest[len(rest) - 6 : -2] if peak else rest
        stress_rows(Grid(vf, 1.0), sf, mf, osf, omf, pf)
        stress_rows(Grid(vc, 3.0), sc, mc, osc, omc, pc)
        if peak:
            (kf, kc, ef), (okf, okc) = rest[:3], rest[-2:]
            okf[0:EARLY] = ef[0:EARLY]
            peak_rows(sf, pf, kf, okf, EARLY, sf.shape[1])
            peak_rows(sc, pc, kc, okc)

    outs = [like(x) for x in (*stress, *memory, *peak)]
    more = (*peak, early) if peak else ()
    out = call(kernel, "stress_bulk", (), (*velocity, *props, *stress, *memory, *more), outs, [], BULK)
    return out[:2], out[2:4], tuple(out[4:])


def velocity_finish(sizes, interp, restrict, halos, props, velocity):
    def kernel(interp, restrict, *rest):
        halos, (pf, pc), (vf, vc), (of, oc), buffers = rest[:5], rest[5:7], rest[7:9], rest[9:11], rest[11:16]
        halo, (lift, gather) = rest[16:20], rest[20:]
        receive(sizes, halos, STRESS_Z, interp, halo, lift)
        velocity_edges(Edges(sizes, True, STRESS_X, STRESS_Z, halo), vf, of, pf)
        velocity_edges(Edges(sizes, False, STRESS_X, STRESS_Z, halo), vc, oc, pc)
        send(sizes, of, oc, VELOCITY_X, VELOCITY_Z, restrict, buffers, gather)

    outs = [like(v) for v in velocity] + packs(sizes)
    out = call(
        kernel, "velocity_finish", (interp, restrict), (*halos, *props, *velocity), outs,
        halo_scratch(sizes) + [gather_scratch(sizes)], 10**7,
    )
    return out[:2], out[2:]


def stress_finish(sizes, interp, restrict, halos, props, stress, memory):
    def kernel(interp, restrict, *rest):
        halos, (pf, pc), (sf, sc, mf, mc), (osf, osc, omf, omc) = rest[:5], rest[5:7], rest[7:11], rest[11:15]
        outgoing, halo, (lift, gather) = rest[15:20], rest[20:24], rest[24:]
        receive(sizes, halos, VELOCITY_Z, interp, halo, lift)
        stress_edges(Edges(sizes, True, VELOCITY_X, VELOCITY_Z, halo), sf, mf, osf, omf, pf)
        stress_edges(Edges(sizes, False, VELOCITY_X, VELOCITY_Z, halo), sc, mc, osc, omc, pc)
        send(sizes, osf, osc, STRESS_X, STRESS_Z, restrict, outgoing, gather)

    outs = [like(x) for x in (*stress, *memory)] + packs(sizes)
    out = call(
        kernel, "stress_finish", (interp, restrict), (*halos, *props, *stress, *memory), outs,
        halo_scratch(sizes) + [gather_scratch(sizes)], 2 * 10**7,
    )
    return out[:2], out[2:4], out[4:]


def last_finish(sizes, interp, halos, props, stress, memory, peak, velocity):
    def kernel(interp, *rest):
        halos, (pf, pc), (sf, sc, mf, mc), (kf, kc), speeds = rest[:5], rest[5:7], rest[7:11], rest[11:13], rest[13:15]
        outs, halo, lift = rest[15:23], rest[23:27], rest[27]
        near, sems = rest[28:34], rest[34]

        def whole(i):
            source = speeds[i] if i < 2 else near[i - 2]
            return pltpu.make_async_copy(source, outs[i], sems.at[i])

        for i in range(2):
            whole(i).start()
        receive(sizes, halos, VELOCITY_Z, interp, halo, lift)
        osf, osc, omf, omc, okf, okc = near

        def store(x):
            for i in (2, 4):
                pltpu.make_async_copy(near[i - 2].at[:, x], outs[i].at[:, x], sems.at[i]).start()

        stress_edges(Edges(sizes, True, VELOCITY_X, VELOCITY_Z, halo), sf, mf, osf, omf, pf, store)
        stress_edges(Edges(sizes, False, VELOCITY_X, VELOCITY_Z, halo), sc, mc, osc, omc, pc)
        for i in (3, 5):
            whole(i).start()
        peak_rows(osf, pf, kf, okf)
        whole(6).start()
        peak_rows(osc, pc, kc, okc)
        whole(7).start()
        for i in range(8):
            whole(i).wait()

    outs = [like(x) for x in (*velocity, *stress, *memory, *peak)]
    scratch = halo_scratch(sizes) + [room(x) for x in (*stress, *memory, *peak)] + [pltpu.SemaphoreType.DMA((8,))]
    out = call(
        kernel, "last_finish", (interp,), (*halos, *props, *stress, *memory, *peak, *velocity), [],
        scratch, 2 * 10**7, far_outs=outs,
    )
    return out[:2], out[2:4], out[4:6], out[6:]


def rotation(low, high, pivot):
    gap = high - low
    twice = pivot + pivot
    square = twice * twice
    length2 = jnp.maximum(gap * gap + square, TINY)
    length = length2 * lax.rsqrt(length2)
    signed = jnp.where(gap >= 0, length, -length)
    middle = 0.5 * (low + high)
    reach = 0.5 * signed
    base = gap + signed

    def turn():
        inverse = lax.rsqrt(base * base + square)
        return base * inverse, twice * inverse

    return middle - reach, middle + reach, turn


def largest_eigenvalue(a, b, c, ab, ac, bc):
    a, b, turn = rotation(a, b, ab)
    cosine, sine = turn()
    ac, bc = cosine * ac - sine * bc, sine * ac + cosine * bc
    for sweep in range(3):
        if sweep > 0:
            a, b, turn = rotation(a, b, ab)
            cosine, sine = turn()
            ac, bc = cosine * ac, sine * ac
        a, c, turn = rotation(a, c, ac)
        cosine, sine = turn()
        ab, bc = -(sine * bc), cosine * bc
        b, c, turn = rotation(b, c, bc)
        if sweep < 2:
            cosine, sine = turn()
            ab, ac = cosine * ab, sine * ab
    return jnp.maximum(jnp.maximum(a, b), c)


def peak_rows(stress, props, peak, out, first=0, end=None, width=2):
    def step(i, carry):
        x = pl.ds(i * width, width)
        xx, yy, zz, xy, xz, yz = [stress[comp, x] for comp in range(6)]
        top = largest_eigenvalue(xx, yy, zz, xy, xz, yz)
        principal = (top - props[ISO, x] * (xx + yy + zz)) * props[SCALE, x]
        out[x] = jnp.maximum(peak[x], principal)
        return carry

    lax.fori_loop(first // width, (end or stress.shape[1]) // width, step, 0)


def exchanged(arrays):
    depO, diag, depE, latO, latE = arrays
    lat, depth = lax.axis_size("lat"), lax.axis_size("depth")

    def swaps(count, first):
        pairs = [(i, (i + 1) % count) for i in range(first, count, 2)]
        return pairs + [(b, a) for a, b in pairs]

    across = [((i + 1) * depth, i * depth + depth - 1) for i in range(lat - 1)]
    depO = lax.ppermute(depO, "depth", swaps(depth, 1))
    diag = lax.ppermute(diag, ("lat", "depth"), across)
    depE = lax.ppermute(depE, "depth", swaps(depth, 0))
    latO = lax.ppermute(latO, "lat", swaps(lat, 1))
    latE = lax.ppermute(latE, "lat", swaps(lat, 0))
    return (depO, diag, depE, latO, latE)


def on_device(
    velocity_fine,
    stress_fine,
    memory_fine,
    peak_fine,
    zone_fine,
    velocity_coarse,
    stress_coarse,
    memory_coarse,
    peak_coarse,
    zone_coarse,
    zone_table,
    interp_weight,
    restrict_weight,
):
    sizes = Sizes(stress_fine.shape[1:], stress_coarse.shape[1:])
    velocity = (velocity_fine, velocity_coarse)
    stress = (stress_fine, stress_coarse)
    memory = (memory_fine, memory_coarse)
    peak = (peak_fine, peak_coarse)
    outgoing = pack_stress(sizes, restrict_weight, *stress)
    for step in range(STEPS):
        halos = exchanged(outgoing)
        if step == 0:
            velocity, props = first_bulk(zone_table, (zone_fine, zone_coarse), stress, velocity)
        else:
            velocity, early = velocity_bulk(stress, props, velocity, peak)
        velocity, outgoing = velocity_finish(
            sizes, interp_weight, restrict_weight, halos, props, velocity
        )
        halos = exchanged(outgoing)
        if step == 0:
            stress, memory, _ = stress_bulk(velocity, props, stress, memory)
        else:
            stress, memory, peak = stress_bulk(velocity, props, stress, memory, peak, early)
        if step + 1 < STEPS:
            stress, memory, outgoing = stress_finish(
                sizes, interp_weight, restrict_weight, halos, props, stress, memory
            )
        else:
            velocity, stress, memory, peak = last_finish(
                sizes, interp_weight, halos, props, stress, memory, peak, velocity
            )
    return (velocity[0], stress[0], memory[0], peak[0], velocity[1], stress[1], memory[1], peak[1])


def solution(mesh):
    field = P(None, "lat", "depth", None)
    scalar = P("lat", "depth", None)
    grid = (field, field, field, scalar)
    return jax.shard_map(
        on_device,
        mesh=mesh,
        in_specs=(*grid, scalar, *grid, scalar, P(), P(), P()),
        out_specs=(*grid, *grid),
        check_vma=False,
    )
```
